256 devices in a mesh: pts: 32 (over z, y_hi, core), cam: 8 (over y_lo, x).
Axes of the slice: x: 4, y: 4 (y_hi: 2, y_lo: 2; y = y_hi * 2 + y_lo), z: 8, core: 2. Of those that a mesh axis runs over, the one named last changes fastest.
Arguments:
- rhs: float32 [8, 256, 576], P('cam', 'pts'), may hold values from -6 to 6
- damp_cam: float32 [8, 256, 576], P('cam', 'pts'), may hold values from 0.2 to 1
- precond: float32 [8, 256, 576], P('cam', 'pts'), may hold values from 0.3 to 3
- cam_jac: float32 [8, 3072, 8, 18, 128], P('cam', 'pts'), may hold values from -0.3125 to 0.3125
- pt_jac: float32 [8, 3072, 8, 6, 128], P('cam', 'pts'), may hold values from -6 to 6
- damp_pt: float32 [8, 3072, 3, 128], P('cam', 'pts'), may hold values from 0.5 to 8
- cam_index: int32 [8, 3072, 8, 128], P('cam', 'pts'), may hold values from 0 to 63
- tile_ids: int32 [8, 3072, 8], P('cam', 'pts'), may hold values from 0 to 511, as said below
- counts: int32 [8, 3072], P('cam', 'pts'), may hold values from 2 to 8, as said below
Outputs:
- solution: float32 [8, 256, 576], P('cam', 'pts')
- residual: float32 [8, 256, 576], P('cam', 'pts')
The draws below stay inside these ranges and needn't reach their ends.
Inputs may be any that keep to these rules, and one draw needn't show every extreme that they name: `tile_ids`: point tile t of a group (t from 0 to 3071) lists only window tiles from (t * 256) // 3072 to that plus 256; entries at or beyond the tile's count are padding within the same range. `counts`: in every group the first point tile has all 8 entries live.
All inputs are finite; a program needn't handle non-finite values.
Results may differ from the reference program's by a relative error of at most 0.0003.
Values sent between devices are 32-bit elements; how exact they have to be, the bound alone decides.
A program may use at most 64 MiB of HBM per device.

```python
import math
import jax
import jax.numpy as jnp
from jax import lax

CAMS = 64
CPAR = 9
PP = 128
SLOTS = 8
ITERS = 3
CT_DEV = 8
PT_DEV = 96
TILE = 576
GROUPS = 8
CT_GROUP = 256
PT_GROUP = 3072
HALF = 128


def draw_tile_ids(key, part):
    position = jnp.arange(PT_GROUP, dtype=jnp.int32)
    start = position * CT_GROUP // PT_GROUP
    offsets = jax.random.randint(key, (GROUPS, PT_GROUP, SLOTS), 0, CT_GROUP + 1)
    offsets = offsets.at[:, 0, 0].set(0)
    offsets = offsets.at[:, PT_GROUP - 1, 0].set(CT_GROUP)
    return (start[None, :, None] + offsets).astype(jnp.int32)


def draw_counts(key, part):
    counts = jax.random.randint(key, (GROUPS, PT_GROUP), 2, SLOTS + 1)
    counts = counts.at[:, 0].set(SLOTS)
    counts = counts.at[:, 1].set(2)
    return counts.astype(jnp.int32)


def touch_ends(drawn, own_key, least, largest):
    dims = drawn.shape
    spot = [jax.random.randint(jax.random.fold_in(own_key, axis), (), 0, dims[axis]) for axis in range(len(dims))]
    drawn = drawn.at[tuple(spot)].set(least)
    longest = dims.index(max(dims))
    spot[longest] = (spot[longest] + 1) % dims[longest]
    return drawn.at[tuple(spot)].set(largest)


def levels(rng, shape, cuts, smallest, high):
    factor_of, own = 1.0, jax.random.fold_in(rng, 6)
    for dim, shards_of in cuts:
        steps = jnp.exp(jax.random.uniform(jax.random.fold_in(own, dim), (shards_of,), jnp.float32, smallest / len(cuts), high / len(cuts)))
        factor_of = factor_of * jnp.repeat(steps, shape[dim] // shards_of).reshape([-1 if axis == dim else 1 for axis in range(len(shape))])
    return factor_of


def bell_draw(own_key, extent, width, bound, split=(), kind=jnp.bfloat16):
    result = width * jax.random.normal(own_key, extent, jnp.float32)
    if split:
        result = result * levels(own_key, extent, split, -0.22, 0.18)
    return jnp.clip(result, -bound, bound).astype(kind)


def setup_inputs(seed: int = 0) -> dict:
    key_of = jax.random.split(jax.random.key(seed), 10)
    rhs = bell_draw(key_of[0], (GROUPS, CT_GROUP, TILE), 1.0, 6.0, ((0, 8), (1, 32)), jnp.float32)
    damp_cam = jnp.clip(jnp.exp(math.log(1.0) - 1.609438 * jax.random.uniform(key_of[1], (GROUPS, CT_GROUP, TILE), jnp.float32) ** levels(key_of[1], (GROUPS, CT_GROUP, TILE), ((0, 8), (1, 32)), -0.2, 0.2)), 0.2, 1.0)
    precond = jnp.clip(jnp.exp(math.log(3.0) - 2.3025851 * jax.random.uniform(key_of[2], (GROUPS, CT_GROUP, TILE), jnp.float32) ** levels(key_of[2], (GROUPS, CT_GROUP, TILE), ((0, 8), (1, 32)), -0.2, 0.2)), 0.3, 3.0)
    cam_jac = bell_draw(key_of[3], (GROUPS, PT_GROUP, SLOTS, 2 * CPAR, PP), (2 * PT_DEV * PP * SLOTS // (CT_DEV * CAMS)) ** -0.5, 0.3125, ((0, 8), (1, 32)), jnp.float32)
    pt_jac = bell_draw(key_of[4], (GROUPS, PT_GROUP, SLOTS, 6, PP), 1.0, 6.0, ((0, 8), (1, 32)), jnp.float32)
    damp_pt = jnp.clip(jnp.exp(math.log(8.0) - 2.7725887 * jax.random.uniform(key_of[5], (GROUPS, PT_GROUP, 3, PP), jnp.float32) ** levels(key_of[5], (GROUPS, PT_GROUP, 3, PP), ((0, 8), (1, 32)), -0.2, 0.2)), 0.5, 8.0)
    cam_index = touch_ends(jax.random.randint(key_of[6], (GROUPS, PT_GROUP, SLOTS, PP), 0, CAMS), jax.random.fold_in(key_of[6], 1), 0, CAMS - 1).astype(jnp.int32)
    tile_ids = draw_tile_ids(jax.random.fold_in(key_of[9], 71), 0)
    counts = draw_counts(jax.random.fold_in(key_of[9], 71), 0)
    return dict(rhs=rhs, damp_cam=damp_cam, precond=precond, cam_jac=cam_jac, pt_jac=pt_jac, damp_pt=damp_pt, cam_index=cam_index, tile_ids=tile_ids, counts=counts)


def point_inverse(pt_jac, counts, damp_pt):
    tiles = pt_jac.shape[0]
    points = pt_jac.shape[-1]
    live = (jnp.arange(SLOTS, dtype=jnp.int32)[None, :] < counts[:, None]).astype(jnp.float32)
    shaped = pt_jac.reshape(tiles, SLOTS, 2, 3, points)
    gram = jnp.sum(live[:, :, None, None, None, None] * shaped[:, :, :, :, None, :] * shaped[:, :, :, None, :, :], axis=(1, 2))
    gram = gram + damp_pt[:, :, None, :] * jnp.eye(3, dtype=jnp.float32)[None, :, :, None]
    first = jnp.roll(jnp.roll(gram, -1, axis=1), -1, axis=2)
    second = jnp.roll(jnp.roll(gram, -2, axis=1), -2, axis=2)
    mixed_one = jnp.roll(jnp.roll(gram, -1, axis=1), -2, axis=2)
    mixed_two = jnp.roll(jnp.roll(gram, -2, axis=1), -1, axis=2)
    cofactor = first * second - mixed_one * mixed_two
    determinant = jnp.sum(gram[:, 0] * cofactor[:, 0], axis=1)
    return cofactor / determinant[:, None, None, :]


def group_term(items):
    window, cam_jac, pt_jac, cam_index, tile_ids, live, inverse = items
    grid = window.reshape(2 * CT_GROUP, CPAR, CAMS)
    params = jnp.arange(CPAR, dtype=jnp.int32)
    picked = grid[tile_ids[:, :, None, None], params[None, None, :, None], cam_index[:, :, None, :]]
    cam_rows = cam_jac.reshape(PT_GROUP, SLOTS, 2, CPAR, PP)
    point_rows = pt_jac.reshape(PT_GROUP, SLOTS, 2, 3, PP)
    masked = live[:, :, None, None]
    residual_rows = jnp.sum(cam_rows * picked[:, :, None], axis=3) * masked
    point_side = jnp.sum(point_rows * residual_rows[:, :, :, None, :], axis=(1, 2))
    solved = jnp.sum(inverse * point_side[:, None, :, :], axis=2)
    errors = (residual_rows - jnp.sum(point_rows * solved[:, None, None, :, :], axis=3)) * masked
    returned = jnp.sum(cam_rows * errors[:, :, :, None, :], axis=2)
    flat_ids = (tile_ids[:, :, None] * CAMS + cam_index).reshape(-1)
    values = jnp.transpose(returned, (0, 1, 3, 2)).reshape(-1, CPAR)
    summed = jax.ops.segment_sum(values, flat_ids, num_segments=2 * CT_GROUP * CAMS)
    return jnp.transpose(summed.reshape(2 * CT_GROUP, CAMS, CPAR), (0, 2, 1)).reshape(2 * CT_GROUP, TILE)


def reference(rhs, damp_cam, precond, cam_jac, pt_jac, damp_pt, cam_index, tile_ids, counts):
    live = (jnp.arange(SLOTS, dtype=jnp.int32)[None, None, :] < counts[:, :, None]).astype(jnp.float32)
    inverse = lax.map(lambda items: point_inverse(items[0], items[1], items[2]), (pt_jac, counts, damp_pt))

    def product(vector):
        lower = jnp.roll(vector, 1, axis=0)[:, HALF:]
        upper = jnp.roll(vector, -1, axis=0)[:, :HALF]
        windows = jnp.concatenate([lower, vector, upper], axis=1)
        partial_value = lax.map(group_term, (windows, cam_jac, pt_jac, cam_index, tile_ids, live, inverse))
        middle = partial_value[:, HALF:HALF + CT_GROUP]
        from_below = jnp.roll(partial_value[:, HALF + CT_GROUP:], 1, axis=0)
        from_above = jnp.roll(partial_value[:, :HALF], -1, axis=0)
        return middle + jnp.concatenate([from_below, from_above], axis=1) + damp_cam * vector

    solution = jnp.zeros(rhs.shape, jnp.float32)
    residual = rhs
    scaled = precond * residual
    direction = scaled
    energy = jnp.sum(residual * scaled)
    for iteration in range(ITERS):
        mapped = product(direction)
        step_size = energy / jnp.sum(direction * mapped)
        solution = solution + step_size * direction
        residual = residual - step_size * mapped
        scaled = precond * residual
        energy_next = jnp.sum(residual * scaled)
        direction = scaled + (energy_next / energy) * direction
        energy = energy_next
    return solution, residual
```

```python
import functools

import jax
import jax.numpy as jnp
from jax import lax
from jax.experimental import pallas as pl
from jax.experimental.pallas import tpu as pltpu
from jax.sharding import PartitionSpec as P

ITERS = 3
CPAR = 9
CAMS = 64
LANES = 128
SCALE = 0.125
MESH = pl.DeviceIdType.MESH
F32 = jnp.float32
BF16 = jnp.bfloat16
NT = (((1,), (1,)), ((), ()))
NN = (((1,), (0,)), ((), ()))


def mm(a, b, dims):
    return lax.dot_general(a, b, dims, preferred_element_type=F32)


def split_two(x):
    hi = x.astype(BF16)
    return hi, (x - hi.astype(F32)).astype(BF16)


def kernel(
    n_pts, n_cam, tiles, slots, ct,
    rhs_ref, damp_ref, precond_ref, ids_col_ref, ids_row_ref, counts_ref,
    cam_jac_ref, pt_jac_ref, damp_pt_ref, cam_index_ref,
    sol_ref, res_ref,
    jac, pjac, dpt, cidx, inv, sel, pick_hot, sum_hot, picked, spread, win_split,
    win, acc, got, mixed, parts, vecs, bases, scal_cam, scal_pts,
    in_sem, wsend, wrecv, fsend, frecv, psend, precv, rsend, rrecv, csend, crecv, osend, orecv,
):
    half = n_pts // 2
    chips = half * n_cam
    reach = half // 2
    span = 2 * reach + 1
    rows = span * 2 * ct
    width = 5 * LANES
    pairs = tiles * slots
    d = lax.axis_index("pts")
    g = lax.axis_index("cam")
    core = lax.rem(d, 2)
    other = 1 - core
    chip = g * half + d // 2

    def at_offset(offset):
        place = lax.rem(chip + (offset + chips), chips)
        return {"pts": lax.rem(place, half) * 2 + core, "cam": place // half}

    partner = {"pts": d + 1 - 2 * core, "cam": g}
    offsets = []
    for far in range(reach, 0, -1):
        offsets += [far, -far]

    loads = [
        pltpu.make_async_copy(pt_jac_ref.at[0], pjac.at[:, :, pl.ds(0, 6), :], in_sem.at[0]),
        pltpu.make_async_copy(damp_pt_ref.at[0], dpt.at[:, pl.ds(0, 3), :], in_sem.at[1]),
        pltpu.make_async_copy(cam_index_ref.at[0], cidx, in_sem.at[2]),
        pltpu.make_async_copy(cam_jac_ref.at[0], jac.at[:, :, pl.ds(0, 2 * CPAR), :], in_sem.at[3]),
    ]
    for load in loads:
        load.start()

    barrier = pltpu.get_barrier_semaphore()

    def greet(device):
        pl.semaphore_signal(barrier, inc=1, device_id=device, device_id_type=MESH)

    for offset in offsets:
        greet(at_offset(offset))
    greet(partner)
    for i in range(1, n_cam):
        greet({"pts": d, "cam": lax.rem(g + i, n_cam)})
    for i in range(1, n_pts):
        greet({"pts": lax.rem(d + i, n_pts), "cam": g})
    pl.semaphore_wait(barrier, len(offsets) + 1 + (n_cam - 1) + (n_pts - 1))

    def send(src, dst, ssem, rsem, device):
        copy = pltpu.make_async_remote_copy(
            src_ref=src, dst_ref=dst, send_sem=ssem, recv_sem=rsem, device_id=device, device_id_type=MESH
        )
        copy.start()
        return copy

    def start_gather(p, value):
        win[p, reach, core] = value
        copies = []
        for offset in offsets:
            slot = reach - offset
            copies.append(
                send(win.at[p, reach, core], win.at[p, slot, core], wsend.at[p, slot], wrecv.at[p, slot], at_offset(offset))
            )
        copies.append(
            send(win.at[p, reach, core], win.at[p, reach, core], fsend.at[p, reach], frecv.at[p, reach], partner)
        )
        return copies

    def finish_gather(p, copies):
        forwards = [copies.pop()]
        for offset, copy in reversed(list(zip(offsets, copies))):
            copy.wait_recv()
            slot = reach - offset
            forwards.append(
                send(win.at[p, slot, core], win.at[p, slot, core], fsend.at[p, slot], frecv.at[p, slot], partner)
            )
        for copy in copies:
            copy.wait_send()
        for copy in forwards:
            copy.wait()

    def reduce_blocks(p):
        swaps = []
        order = offsets + [0]
        for offset in order:
            b = reach + offset
            swaps.append(send(acc.at[p, b, other], got.at[p, b], psend.at[p, b], precv.at[p, b], partner))
        copies = []
        for offset, swap in zip(order, swaps):
            b = reach + offset
            swap.wait_recv()
            total = acc[p, b, core] + got[p, b]
            if offset:
                mixed[p, b] = total
                copies.append(send(mixed.at[p, b], parts.at[p, b], rsend.at[p, b], rrecv.at[p, b], at_offset(offset)))
        for offset, copy in zip(offsets, copies):
            copy.wait_recv()
            total = total + parts[p, reach + offset]
        for swap in swaps:
            swap.wait_send()
        for copy in copies:
            copy.wait_send()
        return total

    def wide(value):
        return jnp.concatenate([value, jnp.zeros((ct, width - value.shape[1]), F32)], axis=1)

    sub = lax.broadcasted_iota(jnp.int32, (slots, LANES), 0)
    lane = lax.broadcasted_iota(jnp.int32, (slots, LANES), 1)
    even = lax.rem(sub, 2) == 0
    low = lane < CAMS
    straight = even == low

    rhs = wide(rhs_ref[0])
    damp = wide(damp_ref[0])
    precond = wide(precond_ref[0])
    vecs[0] = rhs
    scaled = precond * rhs
    bases[0] = scaled
    copies = start_gather(0, scaled)

    shift = (d // 2) * (2 * ct)
    spot = lax.broadcasted_iota(jnp.int32, (16, width), 1)
    spot = jnp.where(spot < rows, spot, spot - rows)

    def pick_rows(i, carry):
        ids = ids_col_ref[pl.ds(i * 16, 16), :] - shift
        hot = jnp.where(spot == ids, 1.0, 0.0).astype(BF16)
        pick_hot[pl.ds(i * 16, 16), :] = hot
        return carry

    lax.fori_loop(0, pairs // 16, pick_rows, 0)
    high = lax.broadcasted_iota(jnp.int32, (16, pairs), 0)

    def sum_rows(i, carry):
        ids = ids_row_ref[...] - shift - i * 16
        hot = jnp.where(high == ids, 1.0, 0.0).astype(BF16)
        sum_hot[pl.ds(i * 16, 16), pl.ds(0, pairs)] = hot
        sum_hot[pl.ds(i * 16, 16), pl.ds(pairs, pairs)] = hot
        return carry

    lax.fori_loop(0, rows // 16, sum_rows, 0)
    loads[0].wait()
    loads[1].wait()
    loads[2].wait()
    jflat = jac.reshape(tiles * slots * 24, LANES)
    pflat = pjac.reshape(tiles * slots * 8, LANES)

    def live_of(t):
        return sub < counts_ref[0, t]

    def point_rows(t):
        return [pflat[pl.ds(t * slots * 8 + r, slots, stride=8), :] for r in range(6)]

    camera = lax.broadcasted_iota(jnp.int32, (CAMS, LANES), 0)

    def prepare(t, carry):
        live = live_of(t)
        p = [jnp.where(live, row, 0.0) for row in point_rows(t)]

        def entry(a, b):
            value = jnp.sum(p[a] * p[b] + p[3 + a] * p[3 + b], axis=0, keepdims=True)
            if a == b:
                value = value + dpt[t, pl.ds(a, 1), :]
            return value

        v00, v01, v02 = entry(0, 0), entry(0, 1), entry(0, 2)
        v11, v12, v22 = entry(1, 1), entry(1, 2), entry(2, 2)
        c00 = v11 * v22 - v12 * v12
        c01 = v12 * v02 - v01 * v22
        c02 = v01 * v12 - v11 * v02
        c11 = v22 * v00 - v02 * v02
        c12 = v02 * v01 - v00 * v12
        c22 = v00 * v11 - v01 * v01
        det = v00 * c00 + v01 * c01 + v02 * c02
        for i, value in enumerate((c00, c01, c02, c11, c12, c22)):
            inv[t, pl.ds(i, 1), :] = value / det
        for k in range(slots):
            index = cidx[t, pl.ds(k, 1), :]
            sel[t, pl.ds(k * CAMS, CAMS), :] = jnp.where(camera == index, 1.0, 0.0).astype(BF16)
        return carry

    lax.fori_loop(0, tiles, prepare, 0)
    loads[3].wait()

    def tile_term(t):
        live = live_of(t)
        index = cidx[t]
        above = index + CAMS
        j_rows = [jflat[pl.ds(t * slots * 24 + r, slots, stride=24), :] for r in range(2 * CPAR)]
        p = point_rows(t)
        found = []
        for j in range(CPAR):
            table = picked[pl.ds(t * slots, slots), pl.ds((j // 2) * LANES, LANES)]
            found.append(
                jnp.take_along_axis(table, above if j % 2 else index, axis=1, mode="promise_in_bounds")
            )
        q = []
        for r in range(2):
            total = j_rows[CPAR * r] * found[0]
            for j in range(1, CPAR):
                total = total + j_rows[CPAR * r + j] * found[j]
            q.append(jnp.where(live, total, 0.0))
        y = [jnp.sum(p[a] * q[0] + p[3 + a] * q[1], axis=0, keepdims=True) for a in range(3)]
        m = [inv[t, pl.ds(i, 1), :] for i in range(6)]
        z = [
            m[0] * y[0] + m[1] * y[1] + m[2] * y[2],
            m[1] * y[0] + m[3] * y[1] + m[4] * y[2],
            m[2] * y[0] + m[4] * y[1] + m[5] * y[2],
        ]
        e = []
        for r in range(2):
            back = p[3 * r] * z[0] + p[3 * r + 1] * z[1] + p[3 * r + 2] * z[2]
            e.append(jnp.where(live, q[r] - back, 0.0))
        given = jnp.concatenate([j_rows[j] * e[0] + j_rows[CPAR + j] * e[1] for j in range(CPAR)], axis=0)
        hi, lo = split_two(given)
        hots = sel[t]
        out = mm(jnp.concatenate([hi, lo], axis=1), jnp.concatenate([hots, hots], axis=1), NT)

        def diagonal(j):
            block = [out[j * slots : (j + 1) * slots, i * LANES : (i + 1) * LANES] for i in range(slots // 2)]
            value = block[-1]
            for i in range(slots // 2 - 2, -1, -1):
                value = jnp.where(sub < 2 * (i + 1), block[i], value)
            return value

        merged = []
        for i in range(0, CPAR, 2):
            first = diagonal(i)
            second = diagonal(i + 1) if i + 1 < CPAR else jnp.zeros_like(first)
            crossed = pltpu.roll(jnp.where(even, second, first), CAMS, 1)
            merged.append(jnp.where(straight, jnp.where(even, first, second), crossed))
        return jnp.concatenate(merged, axis=1)

    together = 4

    def tile_step(i, carry):
        terms = [tile_term(i * together + u) for u in range(together)]
        for u in range(0, together, 2):
            hi, lo = split_two(jnp.concatenate(terms[u : u + 2], axis=0))
            start = pl.multiple_of((i * together + u) * slots, 16)
            spread[pl.ds(start, 16), :] = hi
            spread[pl.ds(pairs + start, 16), :] = lo
        return carry

    for p in range(ITERS):
        finish_gather(p, copies)
        window = win[p].reshape(rows, width)
        hi, lo = split_two(window)
        win_split[pl.ds(0, rows), :] = hi
        win_split[pl.ds(rows, rows), :] = lo

        def pick(i, carry):
            start = pl.multiple_of(i * LANES, LANES)
            picked[pl.ds(start, LANES), :] = mm(pick_hot[pl.ds(start, LANES), pl.ds(0, 2 * rows)], win_split[...], NN)
            return carry

        lax.fori_loop(0, pairs // LANES, pick, 0)
        lax.fori_loop(0, tiles // together, tile_step, 0)
        for i in range(5):
            cut = pl.ds(i * LANES, LANES)
            value = mm(sum_hot[...], spread[:, cut], NN)
            acc[p, :, :, :, cut] = value.reshape(span, 2, ct, LANES)
        total = reduce_blocks(p)
        mapped = SCALE * (total + damp * bases[p])
        vecs[p + 1] = mapped
        if p + 1 < ITERS:
            scaled = precond * mapped
            bases[p + 1] = scaled
            copies = start_gather(p + 1, scaled)

    wanted = [(i, j) for i in range(ITERS) for j in range(i, ITERS + 1)]
    lines = []
    for i, j in wanted:
        product = bases[i] * vecs[j]
        line = product[:, :LANES]
        for n in range(1, 5):
            line = line + product[:, n * LANES : (n + 1) * LANES]
        lines.append(jnp.sum(line, axis=0, keepdims=True))
    lines.append(jnp.zeros((16 - len(lines), LANES), F32))
    scal_cam[g] = jnp.concatenate(lines, axis=0)
    copies = [
        send(scal_cam.at[g], scal_cam.at[g], csend.at[i], crecv.at[i], {"pts": d, "cam": lax.rem(g + i, n_cam)})
        for i in range(1, n_cam)
    ]
    for copy in copies:
        copy.wait()
    total = scal_cam[0]
    for i in range(1, n_cam):
        total = total + scal_cam[i]
    scal_pts[d] = total
    copies = [
        send(scal_pts.at[d], scal_pts.at[d], osend.at[i], orecv.at[i], {"pts": lax.rem(d + i, n_pts), "cam": g})
        for i in range(1, n_pts)
    ]
    for copy in copies:
        copy.wait()
    total = scal_pts[0]
    for i in range(1, n_pts):
        total = total + scal_pts[i]
    sums = jnp.broadcast_to(jnp.sum(total, axis=1, keepdims=True), (16, LANES))
    gram = {}
    for i, (a, b) in enumerate(wanted):
        gram[a, b] = gram[b, a] = sums[i : i + 1, :]

    one = jnp.ones((1, LANES), F32)
    nil = jnp.zeros((1, LANES), F32)
    x = [nil] * ITERS
    r = [one] + [nil] * ITERS
    s = [one] + [nil] * (ITERS - 1)
    energy = gram[0, 0]
    for p in range(ITERS):
        mapped = [nil] + [value * (1.0 / SCALE) for value in s]
        steep = nil
        for i in range(p + 1):
            row = nil
            for j in range(1, p + 2):
                row = row + mapped[j] * gram[i, j]
            steep = steep + s[i] * row
        step = energy / steep
        x = [a + step * b for a, b in zip(x, s)]
        r = [a - step * b for a, b in zip(r, mapped)]
        if p + 1 < ITERS:
            following = nil
            for i in range(p + 2):
                row = nil
                for j in range(p + 2):
                    row = row + r[j] * gram[i, j]
                following = following + r[i] * row
            ratio = following / energy
            s = [a + ratio * b for a, b in zip(r[:ITERS], s)]
            energy = following

    def spread_out(value):
        return jnp.broadcast_to(value[:, :1], (ct, width))

    solution_value = spread_out(x[0]) * bases[0]
    residual_value = spread_out(r[0]) * vecs[0]
    for i in range(1, ITERS):
        solution_value = solution_value + spread_out(x[i]) * bases[i]
    for i in range(1, ITERS + 1):
        residual_value = residual_value + spread_out(r[i]) * vecs[i]
    sol_ref[0] = solution_value[:, : CPAR * CAMS]
    res_ref[0] = residual_value[:, : CPAR * CAMS]


def solution(mesh):
    n_pts, n_cam = mesh.shape["pts"], mesh.shape["cam"]

    def on_device(rhs, damp_cam, precond, cam_jac, pt_jac, damp_pt, cam_index, tile_ids, counts):
        ct = rhs.shape[1]
        tiles, slots = cam_jac.shape[1:3]
        pairs = tiles * slots
        span = n_pts // 2 + 1
        rows = span * 2 * ct
        width = 5 * LANES
        vmem = pl.BlockSpec(memory_space=pltpu.VMEM)
        anywhere = pl.BlockSpec(memory_space=pl.ANY)
        dma = pltpu.SemaphoreType.DMA
        shape = jax.ShapeDtypeStruct(rhs.shape, F32)
        return pl.pallas_call(
            functools.partial(kernel, n_pts, n_cam, tiles, slots, ct),
            out_shape=(shape, shape),
            in_specs=[vmem] * 5 + [pl.BlockSpec(memory_space=pltpu.SMEM)] + [anywhere] * 4,
            out_specs=(vmem, vmem),
            scratch_shapes=[
                pltpu.VMEM((tiles, slots, 24, LANES), F32),
                pltpu.VMEM((tiles, slots, 8, LANES), F32),
                pltpu.VMEM((tiles, 8, LANES), F32),
                pltpu.VMEM((tiles, slots, LANES), jnp.int32),
                pltpu.VMEM((tiles, 8, LANES), F32),
                pltpu.VMEM((tiles, slots * CAMS, LANES), BF16),
                pltpu.VMEM((pairs, width), BF16),
                pltpu.VMEM((rows, 2 * pairs), BF16),
                pltpu.VMEM((pairs, width), F32),
                pltpu.VMEM((2 * pairs, width), BF16),
                pltpu.VMEM((2 * rows, width), BF16),
                pltpu.VMEM((ITERS, span, 2, ct, width), F32),
                pltpu.VMEM((ITERS, span, 2, ct, width), F32),
                pltpu.VMEM((ITERS, span, ct, width), F32),
                pltpu.VMEM((ITERS, span, ct, width), F32),
                pltpu.VMEM((ITERS, span, ct, width), F32),
                pltpu.VMEM((ITERS + 1, ct, width), F32),
                pltpu.VMEM((ITERS, ct, width), F32),
                pltpu.VMEM((n_cam, 16, LANES), F32),
                pltpu.VMEM((n_pts, 16, LANES), F32),
                dma((4,)),
            ]
            + [dma((ITERS, span))] * 8
            + [dma((n_cam,)), dma((n_cam,)), dma((n_pts,)), dma((n_pts,))],
            compiler_params=pltpu.CompilerParams(
                collective_id=0, has_side_effects=True, vmem_limit_bytes=62_000_000
            ),
        )(
            rhs, damp_cam, precond, tile_ids.reshape(pairs, 1), tile_ids.reshape(1, pairs), counts,
            cam_jac, pt_jac, damp_pt, cam_index,
        )

    return jax.shard_map(
        on_device,
        mesh=mesh,
        in_specs=(
            P("cam", "pts", None),
            P("cam", "pts", None),
            P("cam", "pts", None),
            P("cam", "pts", None, None, None),
            P("cam", "pts", None, None, None),
            P("cam", "pts", None, None),
            P("cam", "pts", None, None),
            P("cam", "pts", None),
            P("cam", "pts"),
        ),
        out_specs=(P("cam", "pts", None), P("cam", "pts", None)),
        check_vma=False,
    )
```

```python
import functools

import jax
import jax.numpy as jnp
from jax import lax
from jax.experimental import pallas as pl
from jax.experimental.pallas import tpu as pltpu
from jax.sharding import PartitionSpec as P

ITERS = 3
CPAR = 9
CAMS = 64
LANES = 128
SCALE = 0.125
MESH = pl.DeviceIdType.MESH
F32 = jnp.float32
BF16 = jnp.bfloat16
NT = (((1,), (1,)), ((), ()))
NN = (((1,), (0,)), ((), ()))


def mm(a, b, dims):
    return lax.dot_general(a, b, dims, preferred_element_type=F32)


def split_two(x):
    hi = x.astype(BF16)
    return hi, (x - hi.astype(F32)).astype(BF16)


def kernel(
    n_pts, n_cam, tiles, slots, ct,
    rhs_ref, damp_ref, precond_ref, ids_ref, counts_ref,
    cam_jac_ref, pt_jac_ref, damp_pt_ref, cam_index_ref,
    sol_ref, res_ref,
    jac, pjac, dpt, cidx, inv, sel, pick_hot, sum_hot, picked, spread, win_split, given_split,
    win, acc, got, crossed, crossing, mixed, parts, vecs, bases, scal_cam, scal_pts,
    in_sem, zsend, zrecv, ysend, yrecv, esend, erecv, fsend, frecv,
    asend, arecv, bsend, brecv, rsend, rrecv, csend, crecv, osend, orecv,
):
    layers = n_pts // 4
    quads = layers * n_cam
    reach = layers // 2
    span = 2 * reach + 1
    rows = span * 4 * ct
    width = 5 * LANES
    pairs = tiles * slots
    d = lax.axis_index("pts")
    g = lax.axis_index("cam")
    layer = d // 4
    side = lax.rem(d, 4) // 2
    core = lax.rem(d, 2)
    quad = g * layers + layer

    def at_offset(offset):
        place = lax.rem(quad + (offset + quads), quads)
        return {"pts": lax.rem(place, layers) * 4 + side * 2 + core, "cam": place // layers}

    twin = {"pts": d + 1 - 2 * core, "cam": g}
    across = {"pts": d + 2 - 4 * side, "cam": g}
    offsets = []
    for far in range(reach, 0, -1):
        offsets += [far, -far]
    places = {offset: at_offset(offset) for offset in offsets}

    loads = [
        pltpu.make_async_copy(pt_jac_ref.at[0], pjac, in_sem.at[0]),
        pltpu.make_async_copy(damp_pt_ref.at[0], dpt, in_sem.at[1]),
        pltpu.make_async_copy(cam_index_ref.at[0], cidx, in_sem.at[2]),
        pltpu.make_async_copy(cam_jac_ref.at[0], jac, in_sem.at[3]),
    ]
    for load in loads:
        load.start()

    barrier = pltpu.get_barrier_semaphore()

    def greet(device):
        pl.semaphore_signal(barrier, inc=1, device_id=device, device_id_type=MESH)

    for offset in offsets:
        greet(places[offset])
    for i in range(1, n_cam):
        greet({"pts": d, "cam": lax.rem(g + i, n_cam)})
    for i in range(1, n_pts):
        greet({"pts": lax.rem(d + i, n_pts), "cam": g})
    pl.semaphore_wait(barrier, len(offsets) + (n_cam - 1) + (n_pts - 1))

    def send(src, dst, ssem, rsem, device):
        copy = pltpu.make_async_remote_copy(
            src_ref=src, dst_ref=dst, send_sem=ssem, recv_sem=rsem, device_id=device, device_id_type=MESH
        )
        copy.start()
        return copy

    def forward(p, slot, of_side, ssem, rsem, device):
        block = win.at[p, slot, of_side, core]
        return send(block, block, ssem.at[p, slot], rsem.at[p, slot], device)

    def start_gather(p, value):
        win[p, reach, side, core] = value
        own = win.at[p, reach, side, core]
        copies = {}
        for offset in offsets:
            slot = reach - offset
            copies[slot] = send(
                own, win.at[p, slot, side, core], zsend.at[p, slot], zrecv.at[p, slot], places[offset]
            )
        ys = {reach: forward(p, reach, side, ysend, yrecv, across)}
        es = {reach: forward(p, reach, side, esend, erecv, twin)}
        return copies, ys, es

    def finish_gather(p, started):
        copies, ys, es = started
        order = [reach] + [reach - offset for offset in reversed(offsets)]
        fs = {}
        lag = 3

        def pass_on(slot):
            ys[slot].wait_recv()
            fs[slot] = forward(p, slot, 1 - side, fsend, frecv, twin)

        for n, slot in enumerate(order):
            if n:
                copies[slot].wait_recv()
                ys[slot] = forward(p, slot, side, ysend, yrecv, across)
                es[slot] = forward(p, slot, side, esend, erecv, twin)
            if n >= lag:
                pass_on(order[n - lag])
        for slot in order[-lag:]:
            pass_on(slot)
        for slot in order:
            es[slot].wait_recv()
        for slot in order:
            fs[slot].wait_recv()
        for slot in order:
            if slot in copies:
                copies[slot].wait_send()
            ys[slot].wait_send()
            es[slot].wait_send()
            fs[slot].wait_send()

    def reduce_blocks(p):
        order = [reach + offset for offset in offsets] + [reach]
        swaps = {}
        for slot in order:
            swaps[slot] = send(acc.at[p, slot, :, 1 - core], got.at[p, slot], asend.at[p, slot], arecv.at[p, slot], twin)
        sides = {}
        for slot in order:
            swaps[slot].wait_recv()
            crossed[p, slot] = acc[p, slot, 1 - side, core] + got[p, slot, 1 - side]
            sides[slot] = send(
                crossed.at[p, slot], crossing.at[p, slot], bsend.at[p, slot], brecv.at[p, slot], across
            )
        copies = {}
        for slot in order:
            sides[slot].wait_recv()
            total = acc[p, slot, side, core] + got[p, slot, side] + crossing[p, slot]
            if slot != reach:
                mixed[p, slot] = total
                copies[slot] = send(
                    mixed.at[p, slot], parts.at[p, slot], rsend.at[p, slot], rrecv.at[p, slot], places[slot - reach]
                )
        for slot in order[:-1]:
            copies[slot].wait_recv()
            total = total + parts[p, slot]
        for slot in order:
            swaps[slot].wait_send()
            sides[slot].wait_send()
            if slot in copies:
                copies[slot].wait_send()
        return total

    def wide(value):
        return jnp.concatenate([value, jnp.zeros((ct, width - value.shape[1]), F32)], axis=1)

    sub = lax.broadcasted_iota(jnp.int32, (slots, LANES), 0)
    lane = lax.broadcasted_iota(jnp.int32, (slots, LANES), 1)
    even = lax.rem(sub, 2) == 0
    low = lane < CAMS
    straight = even == low

    rhs = wide(rhs_ref[0])
    damp = wide(damp_ref[0])
    precond = wide(precond_ref[0])
    vecs[0] = rhs
    scaled = precond * rhs
    bases[0] = scaled
    copies = start_gather(0, scaled)

    shift = layer * (4 * ct)
    spot = lax.broadcasted_iota(jnp.int32, (slots, width), 1)
    spot = jnp.where(spot < rows, spot, spot - rows)
    ids = jnp.concatenate([ids_ref[0] - shift, jnp.zeros((slots, LANES - tiles), jnp.int32)], axis=1)

    def pick_rows(i, carry):
        hots = []
        for u in range(2):
            own = jnp.take_along_axis(ids, jnp.full_like(ids, 2 * i + u), axis=1, mode="promise_in_bounds")
            hots.append(jnp.where(spot == own[:, :1], 1.0, 0.0))
        pick_hot[pl.ds(pl.multiple_of(i * 16, 16), 16), :] = jnp.concatenate(hots, axis=0).astype(BF16)
        return carry

    lax.fori_loop(0, pairs // 16, pick_rows, 0)
    for i in range(pairs // LANES):
        hot = pick_hot[pl.ds(i * LANES, LANES), pl.ds(0, 3 * LANES)].astype(F32)
        hot = jnp.transpose(hot)[:rows].astype(BF16)
        sum_hot[:, pl.ds(i * LANES, LANES)] = hot
        sum_hot[:, pl.ds(pairs + i * LANES, LANES)] = hot
    loads[0].wait()
    loads[1].wait()
    loads[2].wait()
    def live_of(t):
        return sub < counts_ref[0, t]

    def point_rows(t):
        return [pjac[t, r] for r in range(6)]

    camera = lax.broadcasted_iota(jnp.int32, (CAMS, LANES), 0)

    def prepare(i, carry):
        sums = [[] for _ in range(6)]
        for u in range(8):
            t = i * 8 + u
            live = live_of(t)
            p = [jnp.where(live, row, 0.0) for row in point_rows(t)]
            for n, (a, b) in enumerate(((0, 0), (0, 1), (0, 2), (1, 1), (1, 2), (2, 2))):
                sums[n].append(jnp.sum(p[a] * p[b] + p[3 + a] * p[3 + b], axis=0, keepdims=True))
            for k in range(slots):
                index = cidx[t, pl.ds(k, 1), :]
                sel[t, pl.ds(k * CAMS, CAMS), :] = jnp.where(camera == index, 1.0, 0.0).astype(BF16)
        here = pl.ds(pl.multiple_of(i * 8, 8), 8)
        v00, v01, v02, v11, v12, v22 = [jnp.concatenate(part, axis=0) for part in sums]
        v00 = v00 + dpt[0, here, :]
        v11 = v11 + dpt[1, here, :]
        v22 = v22 + dpt[2, here, :]
        c00 = v11 * v22 - v12 * v12
        c01 = v12 * v02 - v01 * v22
        c02 = v01 * v12 - v11 * v02
        c11 = v22 * v00 - v02 * v02
        c12 = v02 * v01 - v00 * v12
        c22 = v00 * v11 - v01 * v01
        det = v00 * c00 + v01 * c01 + v02 * c02
        for n, value in enumerate((c00, c01, c02, c11, c12, c22)):
            inv[n, here, :] = value / det
        return carry

    lax.fori_loop(0, tiles // 8, prepare, 0)
    loads[3].wait()

    def observe(t, u):
        live = live_of(t)
        index = cidx[t]
        above = index + CAMS
        j_rows = [jac[t, r] for r in range(2 * CPAR)]
        p = point_rows(t)
        found = []
        for j in range(CPAR):
            table = picked[pl.ds(t * slots, slots), pl.ds((j // 2) * LANES, LANES)]
            found.append(
                jnp.take_along_axis(table, above if j % 2 else index, axis=1, mode="promise_in_bounds")
            )
        q = []
        for r in range(2):
            total = j_rows[CPAR * r] * found[0]
            for j in range(1, CPAR):
                total = total + j_rows[CPAR * r + j] * found[j]
            q.append(jnp.where(live, total, 0.0))
        y = [jnp.sum(p[a] * q[0] + p[3 + a] * q[1], axis=0, keepdims=True) for a in range(3)]
        m = [inv[n, pl.ds(t, 1), :] for n in range(6)]
        z = [
            m[0] * y[0] + m[1] * y[1] + m[2] * y[2],
            m[1] * y[0] + m[3] * y[1] + m[4] * y[2],
            m[2] * y[0] + m[4] * y[1] + m[5] * y[2],
        ]
        e = []
        for r in range(2):
            back = p[3 * r] * z[0] + p[3 * r + 1] * z[1] + p[3 * r + 2] * z[2]
            e.append(jnp.where(live, q[r] - back, 0.0))
        given = jnp.concatenate([j_rows[j] * e[0] + j_rows[CPAR + j] * e[1] for j in range(CPAR)], axis=0)
        hi, lo = split_two(given)
        given_split[u] = jnp.concatenate([hi, lo], axis=1)
        return q[0] * e[0] + q[1] * e[1]

    def camera_sums(t, u):
        hots = sel[t]
        out = mm(given_split[u], jnp.concatenate([hots, hots], axis=1), NT)

        def diagonal(j):
            block = [out[j * slots : (j + 1) * slots, i * LANES : (i + 1) * LANES] for i in range(slots // 2)]
            value = block[-1]
            for i in range(slots // 2 - 2, -1, -1):
                value = jnp.where(sub < 2 * (i + 1), block[i], value)
            return value

        merged = []
        for i in range(0, CPAR, 2):
            first = diagonal(i)
            second = diagonal(i + 1) if i + 1 < CPAR else jnp.zeros_like(first)
            turned = pltpu.roll(jnp.where(even, second, first), CAMS, 1)
            merged.append(jnp.where(straight, jnp.where(even, first, second), turned))
        return jnp.concatenate(merged, axis=1)

    together = 4
    steps = tiles // together

    def gather_step(i, bend):
        for u in range(together):
            bend = bend + observe(i * together + u, u)
        return bend

    def sum_step(i):
        terms = [camera_sums(i * together + u, u) for u in range(together)]
        for u in range(0, together, 2):
            hi, lo = split_two(jnp.concatenate(terms[u : u + 2], axis=0))
            start = pl.multiple_of((i * together + u) * slots, 16)
            spread[pl.ds(start, 16), :] = hi
            spread[pl.ds(pairs + start, 16), :] = lo

    def both_steps(i, bend):
        sum_step(i - 1)
        return gather_step(i, bend)

    wanted = [(i, j) for j in range(ITERS) for i in range(j + 1)]

    def lane_sums(product):
        line = product[:, :LANES]
        for n in range(1, 5):
            line = line + product[:, n * LANES : (n + 1) * LANES]
        return line

    def start_sums(bend):
        lines = [lane_sums(bases[i] * vecs[j]) for i, j in wanted]
        last = bases[ITERS - 1]
        lines.append(SCALE * (bend + lane_sums(damp * last * last)))
        lines = [jnp.sum(line, axis=0, keepdims=True) for line in lines]
        lines.append(jnp.zeros((8 - len(lines), LANES), F32))
        scal_cam[g] = jnp.concatenate(lines, axis=0)
        return [
            send(scal_cam.at[g], scal_cam.at[g], csend.at[i], crecv.at[i], {"pts": d, "cam": lax.rem(g + i, n_cam)})
            for i in range(1, n_cam)
        ]

    def cross_sums(copies):
        for copy in copies:
            copy.wait()
        total = scal_cam[0]
        for i in range(1, n_cam):
            total = total + scal_cam[i]
        scal_pts[d] = total
        return [
            send(scal_pts.at[d], scal_pts.at[d], osend.at[i], orecv.at[i], {"pts": lax.rem(d + i, n_pts), "cam": g})
            for i in range(1, n_pts)
        ]

    for p in range(ITERS):
        finish_gather(p, copies)
        window = win[p].reshape(rows, width)
        hi, lo = split_two(window)
        win_split[pl.ds(0, rows), :] = hi
        win_split[pl.ds(rows, rows), :] = lo

        def pick(i, carry):
            start = pl.multiple_of(i * LANES, LANES)
            picked[pl.ds(start, LANES), :] = mm(pick_hot[pl.ds(start, LANES), pl.ds(0, 2 * rows)], win_split[...], NN)
            return carry

        lax.fori_loop(0, pairs // LANES, pick, 0)
        bend = gather_step(0, jnp.zeros((slots, LANES), F32))
        bend = lax.fori_loop(1, steps, both_steps, bend)
        sum_step(steps - 1)
        if p + 1 == ITERS:
            started = start_sums(bend)
        for i in range(5):
            cut = pl.ds(i * LANES, LANES)
            value = mm(sum_hot[...], spread[:, cut], NN)
            acc[p, :, :, :, :, cut] = value.reshape(span, 2, 2, ct, LANES)
        if p + 1 == ITERS:
            started = cross_sums(started)
        total = reduce_blocks(p)
        mapped = SCALE * (total + damp * bases[p])
        vecs[p + 1] = mapped
        if p + 1 < ITERS:
            scaled = precond * mapped
            bases[p + 1] = scaled
            copies = start_gather(p + 1, scaled)

    for copy in started:
        copy.wait()
    total = scal_pts[0]
    for i in range(1, n_pts):
        total = total + scal_pts[i]
    sums = jnp.broadcast_to(jnp.sum(total, axis=1, keepdims=True), (8, LANES))
    gram = {}
    for i, (a, b) in enumerate(wanted):
        gram[a, b] = gram[b, a] = sums[i : i + 1, :]
    for i in range(ITERS - 1):
        gram[i, ITERS] = gram[i + 1, ITERS - 1]
    gram[ITERS - 1, ITERS] = sums[len(wanted) : len(wanted) + 1, :]

    one = jnp.ones((1, LANES), F32)
    nil = jnp.zeros((1, LANES), F32)
    x = [nil] * ITERS
    r = [one] + [nil] * ITERS
    s = [one] + [nil] * (ITERS - 1)
    energy = gram[0, 0]
    for p in range(ITERS):
        mapped = [nil] + [value * (1.0 / SCALE) for value in s]
        steep = nil
        for i in range(p + 1):
            row = nil
            for j in range(1, p + 2):
                row = row + mapped[j] * gram[i, j]
            steep = steep + s[i] * row
        step = energy / steep
        x = [a + step * b for a, b in zip(x, s)]
        r = [a - step * b for a, b in zip(r, mapped)]
        if p + 1 < ITERS:
            following = nil
            for i in range(p + 2):
                row = nil
                for j in range(p + 2):
                    row = row + r[j] * gram[i, j]
                following = following + r[i] * row
            ratio = following / energy
            s = [a + ratio * b for a, b in zip(r[:ITERS], s)]
            energy = following

    def spread_out(value):
        return jnp.broadcast_to(value[:, :1], (ct, width))

    solution_value = spread_out(x[0]) * bases[0]
    residual_value = spread_out(r[0]) * vecs[0]
    for i in range(1, ITERS):
        solution_value = solution_value + spread_out(x[i]) * bases[i]
    for i in range(1, ITERS + 1):
        residual_value = residual_value + spread_out(r[i]) * vecs[i]
    sol_ref[0] = solution_value[:, : CPAR * CAMS]
    res_ref[0] = residual_value[:, : CPAR * CAMS]


def solution(mesh):
    n_pts, n_cam = mesh.shape["pts"], mesh.shape["cam"]

    def on_device(rhs, damp_cam, precond, cam_jac, pt_jac, damp_pt, cam_index, tile_ids, counts):
        ct = rhs.shape[1]
        tiles, slots = cam_jac.shape[1:3]
        pairs = tiles * slots
        span = n_pts // 4 + 1
        rows = span * 4 * ct
        width = 5 * LANES
        vmem = pl.BlockSpec(memory_space=pltpu.VMEM)
        anywhere = pl.BlockSpec(memory_space=pl.ANY)
        dma = pltpu.SemaphoreType.DMA
        shape = jax.ShapeDtypeStruct(rhs.shape, F32)
        return pl.pallas_call(
            functools.partial(kernel, n_pts, n_cam, tiles, slots, ct),
            out_shape=(shape, shape),
            in_specs=[vmem] * 4 + [pl.BlockSpec(memory_space=pltpu.SMEM)] + [anywhere] * 4,
            out_specs=(vmem, vmem),
            scratch_shapes=[
                pltpu.VMEM((tiles, 2 * CPAR, slots, LANES), F32),
                pltpu.VMEM((tiles, 6, slots, LANES), F32),
                pltpu.VMEM((3, tiles, LANES), F32),
                pltpu.VMEM((tiles, slots, LANES), jnp.int32),
                pltpu.VMEM((6, tiles, LANES), F32),
                pltpu.VMEM((tiles, slots * CAMS, LANES), BF16),
                pltpu.VMEM((pairs, width), BF16),
                pltpu.VMEM((rows, 2 * pairs), BF16),
                pltpu.VMEM((pairs, width), F32),
                pltpu.VMEM((2 * pairs, width), BF16),
                pltpu.VMEM((2 * rows, width), BF16),
                pltpu.VMEM((4, CPAR * slots, 2 * LANES), BF16),
                pltpu.VMEM((ITERS, span, 2, 2, ct, width), F32),
                pltpu.VMEM((ITERS, span, 2, 2, ct, width), F32),
                pltpu.VMEM((ITERS, span, 2, ct, width), F32),
                pltpu.VMEM((ITERS, span, ct, width), F32),
                pltpu.VMEM((ITERS, span, ct, width), F32),
                pltpu.VMEM((ITERS, span, ct, width), F32),
                pltpu.VMEM((ITERS, span, ct, width), F32),
                pltpu.VMEM((ITERS + 1, ct, width), F32),
                pltpu.VMEM((ITERS, ct, width), F32),
                pltpu.VMEM((n_cam, 8, LANES), F32),
                pltpu.VMEM((n_pts, 8, LANES), F32),
                dma((4,)),
            ]
            + [dma((ITERS, span))] * 14
            + [dma((n_cam,)), dma((n_cam,)), dma((n_pts,)), dma((n_pts,))],
            compiler_params=pltpu.CompilerParams(
                collective_id=0, has_side_effects=True, vmem_limit_bytes=62_000_000
            ),
        )(
            rhs, damp_cam, precond, jnp.swapaxes(tile_ids, 1, 2), counts,
            jnp.swapaxes(cam_jac, 2, 3), jnp.swapaxes(pt_jac, 2, 3), jnp.swapaxes(damp_pt, 1, 2), cam_index,
        )

    return jax.shard_map(
        on_device,
        mesh=mesh,
        in_specs=(
            P("cam", "pts", None),
            P("cam", "pts", None),
            P("cam", "pts", None),
            P("cam", "pts", None, None, None),
            P("cam", "pts", None, None, None),
            P("cam", "pts", None, None),
            P("cam", "pts", None, None),
            P("cam", "pts", None),
            P("cam", "pts"),
        ),
        out_specs=(P("cam", "pts", None), P("cam", "pts", None)),
        check_vma=False,
    )
```

```python
import functools

import jax
import jax.numpy as jnp
from jax import lax
from jax.experimental import pallas as pl
from jax.experimental.pallas import tpu as pltpu
from jax.sharding import PartitionSpec as P

ITERS = 3
CPAR = 9
CAMS = 64
LANES = 128
SCALE = 0.125
TOG = 8
MESH = pl.DeviceIdType.MESH
F32 = jnp.float32
BF16 = jnp.bfloat16
NT = (((1,), (1,)), ((), ()))
NN = (((1,), (0,)), ((), ()))


def mm(a, b, dims):
    return lax.dot_general(a, b, dims, preferred_element_type=F32)


def split_two(x):
    hi = x.astype(BF16)
    return hi, (x - hi.astype(F32)).astype(BF16)


def kernel(
    n_pts, n_cam, tiles, slots, ct,
    rhs_ref, damp_ref, precond_ref, ids_ref, counts_ref,
    cam_jac_ref, pt_jac_ref, damp_pt_ref, cam_index_ref,
    sol_ref, res_ref,
    jac, pjac, dpt, cidx, inv, sel, pick_hot, sum_hot, picked, spread, win_split, given_split,
    win, acc, got, mixed, parts, vecs, bases, scal_cam, scal_pts,
    in_sem, wsend, wrecv, fsend, frecv, psend, precv, rsend, rrecv, csend, crecv, osend, orecv,
):
    half = n_pts // 2
    chips = half * n_cam
    reach = half // 2
    span = 2 * reach + 1
    rows = span * 2 * ct
    width = 5 * LANES
    used = CPAR * CAMS * ct // LANES
    pairs = tiles * slots
    d = lax.axis_index("pts")
    g = lax.axis_index("cam")
    core = lax.rem(d, 2)
    other = 1 - core
    chip = g * half + d // 2

    def at_offset(offset):
        place = lax.rem(chip + (offset + chips), chips)
        return {"pts": lax.rem(place, half) * 2 + core, "cam": place // half}

    twin = {"pts": d + 1 - 2 * core, "cam": g}
    offsets = []
    for far in range(reach, 0, -1):
        offsets += [far, -far]
    places = {offset: at_offset(offset) for offset in offsets}

    loads = [
        pltpu.make_async_copy(pt_jac_ref.at[0], pjac, in_sem.at[0]),
        pltpu.make_async_copy(damp_pt_ref.at[0], dpt, in_sem.at[1]),
        pltpu.make_async_copy(cam_index_ref.at[0], cidx, in_sem.at[2]),
        pltpu.make_async_copy(cam_jac_ref.at[0], jac, in_sem.at[3]),
    ]
    for load in loads:
        load.start()

    barrier = pltpu.get_barrier_semaphore()

    def greet(device):
        pl.semaphore_signal(barrier, inc=1, device_id=device, device_id_type=MESH)

    for offset in offsets:
        greet(places[offset])
    for i in range(1, n_cam):
        greet({"pts": d, "cam": lax.rem(g + i, n_cam)})
    for i in range(1, n_pts):
        greet({"pts": lax.rem(d + i, n_pts), "cam": g})
    pl.semaphore_wait(barrier, len(offsets) + (n_cam - 1) + (n_pts - 1))

    tail = []

    def send(src, dst, ssem, rsem, device):
        copy = pltpu.make_async_remote_copy(
            src_ref=src, dst_ref=dst, send_sem=ssem, recv_sem=rsem, device_id=device, device_id_type=MESH
        )
        copy.start()
        tail.append(copy)
        return copy

    def block(ref, *index):
        return ref.at[(*index, pl.ds(0, used))]

    def start_gather(p, value):
        win[p, reach, core] = value
        own = block(win, p, reach, core)
        copies = []
        for offset in offsets:
            slot = reach - offset
            copies.append(send(own, block(win, p, slot, core), wsend.at[p, slot], wrecv.at[p, slot], places[offset]))
        copies.append(send(own, own, fsend.at[p, reach], frecv.at[p, reach], twin))
        return copies

    def finish_gather(p, copies):
        forwards = [copies.pop()]
        for offset, copy in reversed(list(zip(offsets, copies))):
            copy.wait_recv()
            slot = reach - offset
            here = block(win, p, slot, core)
            forwards.append(send(here, here, fsend.at[p, slot], frecv.at[p, slot], twin))
        for copy in forwards:
            copy.wait_recv()

    def reduce_blocks(p):
        swaps = []
        order = offsets + [0]
        for offset in order:
            b = reach + offset
            swaps.append(send(block(acc, p, b, other), block(got, p, b), psend.at[p, b], precv.at[p, b], twin))
        copies = []
        for offset, swap in zip(order, swaps):
            b = reach + offset
            swap.wait_recv()
            total = acc[p, b, core] + got[p, b]
            if offset:
                mixed[p, b] = total
                copies.append(
                    send(block(mixed, p, b), block(parts, p, b), rsend.at[p, b], rrecv.at[p, b], places[offset])
                )
        for offset, copy in zip(offsets, copies):
            copy.wait_recv()
            total = total + parts[p, reach + offset]
        return jnp.where(filled, total, 0.0)

    sub = lax.broadcasted_iota(jnp.int32, (slots, LANES), 0)
    lane = lax.broadcasted_iota(jnp.int32, (slots, LANES), 1)
    low = lane < CAMS
    early = lax.rem(sub, 4) < 2
    aligned = early == low
    top = sub < 4
    filled = lax.broadcasted_iota(jnp.int32, (5 * ct, LANES), 0) < used

    def pack_last(x):
        return jnp.where(low, x, pltpu.roll(pltpu.roll(x, 4, 0), CAMS, 1))

    def unpack_last(x):
        return jnp.where(top, x, pltpu.roll(pltpu.roll(x, 4, 0), CAMS, 1))

    def packed(value):
        groups = [value[:, n * LANES : (n + 1) * LANES] for n in range(4)]
        ending = jnp.concatenate([value[:, 4 * LANES :], jnp.zeros((ct, CAMS), F32)], axis=1)
        return jnp.concatenate(groups + [jnp.where(top, pack_last(ending), 0.0)], axis=0)

    def unpacked(value):
        groups = [value[n * ct : (n + 1) * ct] for n in range(4)]
        return jnp.concatenate(groups + [unpack_last(value[4 * ct :])[:, :CAMS]], axis=1)

    rhs = packed(rhs_ref[0])
    damp = packed(damp_ref[0])
    precond = packed(precond_ref[0])
    vecs[0] = rhs
    scaled = precond * rhs
    bases[0] = scaled
    copies = start_gather(0, scaled)

    shift = (d // 2) * (2 * ct)
    spot = lax.broadcasted_iota(jnp.int32, (slots, width), 1)
    spot = jnp.where(spot < rows, spot, spot - rows)
    ids = jnp.concatenate([ids_ref[0] - shift, jnp.zeros((slots, LANES - tiles), jnp.int32)], axis=1)

    def pick_rows(i, carry):
        hots = []
        for u in range(2):
            own = jnp.take_along_axis(ids, jnp.full_like(ids, 2 * i + u), axis=1, mode="promise_in_bounds")
            hots.append(jnp.where(spot == own[:, :1], 1.0, 0.0))
        pick_hot[pl.ds(pl.multiple_of(i * 16, 16), 16), :] = jnp.concatenate(hots, axis=0).astype(BF16)
        return carry

    lax.fori_loop(0, pairs // 16, pick_rows, 0)
    for i in range(pairs // LANES):
        hot = pick_hot[pl.ds(i * LANES, LANES), pl.ds(0, 3 * LANES)].astype(F32)
        hot = jnp.transpose(hot)[:rows].astype(BF16)
        sum_hot[:, pl.ds(i * LANES, LANES)] = hot
        sum_hot[:, pl.ds(pairs + i * LANES, LANES)] = hot
    loads[0].wait()
    loads[1].wait()
    loads[2].wait()
    def live_of(t):
        return sub < counts_ref[0, t]

    def point_rows(t):
        return [pjac[t, r] for r in range(6)]

    camera = lax.broadcasted_iota(jnp.int32, (CAMS, LANES), 0)

    def prepare(i, carry):
        sums = [[] for _ in range(6)]
        for u in range(8):
            t = i * 8 + u
            live = live_of(t)
            p = [jnp.where(live, row, 0.0) for row in point_rows(t)]
            for n, (a, b) in enumerate(((0, 0), (0, 1), (0, 2), (1, 1), (1, 2), (2, 2))):
                sums[n].append(jnp.sum(p[a] * p[b] + p[3 + a] * p[3 + b], axis=0, keepdims=True))
            for k in range(slots):
                index = cidx[t, pl.ds(k, 1), :]
                hot = jnp.where(camera == index, 1.0, 0.0).astype(BF16)
                sel[t, pl.ds((k // 2) * CAMS, CAMS), pl.ds((k % 2) * LANES, LANES)] = hot
        here = pl.ds(pl.multiple_of(i * 8, 8), 8)
        v00, v01, v02, v11, v12, v22 = [jnp.concatenate(part, axis=0) for part in sums]
        v00 = v00 + dpt[0, here, :]
        v11 = v11 + dpt[1, here, :]
        v22 = v22 + dpt[2, here, :]
        c00 = v11 * v22 - v12 * v12
        c01 = v12 * v02 - v01 * v22
        c02 = v01 * v12 - v11 * v02
        c11 = v22 * v00 - v02 * v02
        c12 = v02 * v01 - v00 * v12
        c22 = v00 * v11 - v01 * v01
        det = v00 * c00 + v01 * c01 + v02 * c02
        for n, value in enumerate((c00, c01, c02, c11, c12, c22)):
            inv[n, here, :] = value / det
        return carry

    lax.fori_loop(0, tiles // 8, prepare, 0)
    loads[3].wait()

    together = TOG
    lower = 80
    parity = lax.rem(lax.broadcasted_iota(jnp.int32, (CPAR * slots, LANES), 0), 2)
    odd_rows = parity.astype(F32).astype(BF16)
    even_rows = (1 - parity).astype(F32).astype(BF16)
    for u in range(together):
        given_split[u, pl.ds(64, 16), :] = jnp.zeros((16, 2 * LANES), BF16)
        given_split[u, pl.ds(lower + 64, 16), :] = jnp.zeros((16, 2 * LANES), BF16)

    def observe(t, u):
        live = live_of(t)
        index = cidx[t]
        above = index + CAMS
        j_rows = [jac[t, r] for r in range(2 * CPAR)]
        p = point_rows(t)
        found = []
        for j in range(CPAR):
            table = picked[pl.ds(t * slots, slots), pl.ds((j // 2) * LANES, LANES)]
            found.append(
                jnp.take_along_axis(table, above if j % 2 else index, axis=1, mode="promise_in_bounds")
            )
        q = []
        for r in range(2):
            total = j_rows[CPAR * r] * found[0]
            for j in range(1, CPAR):
                total = total + j_rows[CPAR * r + j] * found[j]
            q.append(jnp.where(live, total, 0.0))
        y = [jnp.sum(p[a] * q[0] + p[3 + a] * q[1], axis=0, keepdims=True) for a in range(3)]
        m = [inv[n, pl.ds(t, 1), :] for n in range(6)]
        z = [
            m[0] * y[0] + m[1] * y[1] + m[2] * y[2],
            m[1] * y[0] + m[3] * y[1] + m[4] * y[2],
            m[2] * y[0] + m[4] * y[1] + m[5] * y[2],
        ]
        e = []
        for r in range(2):
            back = p[3 * r] * z[0] + p[3 * r + 1] * z[1] + p[3 * r + 2] * z[2]
            e.append(jnp.where(live, q[r] - back, 0.0))
        given = jnp.concatenate([j_rows[j] * e[0] + j_rows[CPAR + j] * e[1] for j in range(CPAR)], axis=0)
        hi, lo = split_two(given)
        heights = CPAR * slots
        given_split[u, pl.ds(0, heights), :] = jnp.concatenate([hi * even_rows, hi * odd_rows], axis=1)
        given_split[u, pl.ds(lower, heights), :] = jnp.concatenate([lo * even_rows, lo * odd_rows], axis=1)
        return q[0] * e[0] + q[1] * e[1]

    def camera_sums(t, u):
        out = mm(given_split[u], sel[t], NT)

        def diagonal(j):
            both = []
            for n in range(slots // 4):
                cut = slice(n * LANES, (n + 1) * LANES)
                both.append(
                    out[j * slots : (j + 1) * slots, cut] + out[lower + j * slots : lower + (j + 1) * slots, cut]
                )
            return jnp.where(top, both[0], both[1])

        merged = []
        for i in range(0, CPAR, 2):
            first = diagonal(i)
            second = diagonal(i + 1) if i + 1 < CPAR else jnp.zeros_like(first)
            turned = pltpu.roll(jnp.where(early, second, first), CAMS, 1)
            merged.append(jnp.where(aligned, jnp.where(early, first, second), turned))
        return jnp.concatenate(merged, axis=1)

    steps = tiles // together

    def gather_step(i, bend):
        for u in range(together):
            bend = bend + observe(i * together + u, u)
        return bend

    def sum_step(i):
        terms = [camera_sums(i * together + u, u) for u in range(together)]
        for u in range(0, together, 2):
            hi, lo = split_two(jnp.concatenate(terms[u : u + 2], axis=0))
            start = pl.multiple_of((i * together + u) * slots, 16)
            spread[pl.ds(start, 16), :] = hi
            spread[pl.ds(pairs + start, 16), :] = lo

    def both_steps(i, bend):
        sum_step(i - 1)
        return gather_step(i, bend)

    wanted = [(i, j) for j in range(ITERS) for i in range(j + 1)]

    def lane_sums(product):
        line = product[:ct]
        for n in range(1, 5):
            line = line + product[n * ct : (n + 1) * ct]
        return line

    def start_sums(bend):
        lines = [lane_sums(bases[i] * vecs[j]) for i, j in wanted]
        last = bases[ITERS - 1]
        lines.append(SCALE * (bend + lane_sums(damp * last * last)))
        lines = [jnp.sum(line, axis=0, keepdims=True) for line in lines]
        lines.append(jnp.zeros((8 - len(lines), LANES), F32))
        scal_cam[g] = jnp.concatenate(lines, axis=0)
        return [
            send(scal_cam.at[g], scal_cam.at[g], csend.at[i], crecv.at[i], {"pts": d, "cam": lax.rem(g + i, n_cam)})
            for i in range(1, n_cam)
        ]

    def cross_sums(copies):
        for copy in copies:
            copy.wait_recv()
        total = scal_cam[0]
        for i in range(1, n_cam):
            total = total + scal_cam[i]
        scal_pts[d] = total
        return [
            send(scal_pts.at[d], scal_pts.at[d], osend.at[i], orecv.at[i], {"pts": lax.rem(d + i, n_pts), "cam": g})
            for i in range(1, n_pts)
        ]

    for p in range(ITERS):
        finish_gather(p, copies)
        for n in range(5):
            window = win[p, :, :, pl.ds(n * ct, ct), :].reshape(rows, LANES)
            if n == 4:
                window = jnp.concatenate(
                    [unpack_last(window[i * ct : (i + 1) * ct]) for i in range(2 * span)], axis=0
                )
            hi, lo = split_two(window)
            cut = pl.ds(n * LANES, LANES)
            win_split[pl.ds(0, rows), cut] = hi
            win_split[pl.ds(rows, rows), cut] = lo

        def pick(i, carry):
            start = pl.multiple_of(i * LANES, LANES)
            picked[pl.ds(start, LANES), :] = mm(pick_hot[pl.ds(start, LANES), pl.ds(0, 2 * rows)], win_split[...], NN)
            return carry

        lax.fori_loop(0, pairs // LANES, pick, 0)
        bend = gather_step(0, jnp.zeros((slots, LANES), F32))
        bend = lax.fori_loop(1, steps, both_steps, bend)
        sum_step(steps - 1)
        if p + 1 == ITERS:
            started = start_sums(bend)
        for i in range(5):
            cut = pl.ds(i * LANES, LANES)
            value = mm(sum_hot[...], spread[:, cut], NN)
            if i == 4:
                value = jnp.concatenate([pack_last(value[n * ct : (n + 1) * ct]) for n in range(2 * span)], axis=0)
            acc[p, :, :, pl.ds(i * ct, ct), :] = value.reshape(span, 2, ct, LANES)
        if p + 1 == ITERS:
            started = cross_sums(started)
        total = reduce_blocks(p)
        mapped = SCALE * (total + damp * bases[p])
        vecs[p + 1] = mapped
        if p + 1 < ITERS:
            scaled = precond * mapped
            bases[p + 1] = scaled
            copies = start_gather(p + 1, scaled)

    for copy in started:
        copy.wait_recv()
    total = scal_pts[0]
    for i in range(1, n_pts):
        total = total + scal_pts[i]
    sums = jnp.broadcast_to(jnp.sum(total, axis=1, keepdims=True), (8, LANES))
    gram = {}
    for i, (a, b) in enumerate(wanted):
        gram[a, b] = gram[b, a] = sums[i : i + 1, :]
    for i in range(ITERS - 1):
        gram[i, ITERS] = gram[i + 1, ITERS - 1]
    gram[ITERS - 1, ITERS] = sums[len(wanted) : len(wanted) + 1, :]

    one = jnp.ones((1, LANES), F32)
    nil = jnp.zeros((1, LANES), F32)
    x = [nil] * ITERS
    r = [one] + [nil] * ITERS
    s = [one] + [nil] * (ITERS - 1)
    energy = gram[0, 0]
    for p in range(ITERS):
        mapped = [nil] + [value * (1.0 / SCALE) for value in s]
        steep = nil
        for i in range(p + 1):
            row = nil
            for j in range(1, p + 2):
                row = row + mapped[j] * gram[i, j]
            steep = steep + s[i] * row
        step = energy / steep
        x = [a + step * b for a, b in zip(x, s)]
        r = [a - step * b for a, b in zip(r, mapped)]
        if p + 1 < ITERS:
            following = nil
            for i in range(p + 2):
                row = nil
                for j in range(p + 2):
                    row = row + r[j] * gram[i, j]
                following = following + r[i] * row
            ratio = following / energy
            s = [a + ratio * b for a, b in zip(r[:ITERS], s)]
            energy = following

    def spread_out(value):
        return jnp.broadcast_to(value, (5 * ct, LANES))

    solution_value = spread_out(x[0]) * bases[0]
    residual_value = spread_out(r[0]) * vecs[0]
    for i in range(1, ITERS):
        solution_value = solution_value + spread_out(x[i]) * bases[i]
    for i in range(1, ITERS + 1):
        residual_value = residual_value + spread_out(r[i]) * vecs[i]
    for copy in tail:
        copy.wait_send()
    sol_ref[0] = unpacked(solution_value)
    res_ref[0] = unpacked(residual_value)


def solution(mesh):
    n_pts, n_cam = mesh.shape["pts"], mesh.shape["cam"]

    def on_device(rhs, damp_cam, precond, cam_jac, pt_jac, damp_pt, cam_index, tile_ids, counts):
        ct = rhs.shape[1]
        tiles, slots = cam_jac.shape[1:3]
        pairs = tiles * slots
        span = n_pts // 2 + 1
        rows = span * 2 * ct
        width = 5 * LANES
        vmem = pl.BlockSpec(memory_space=pltpu.VMEM)
        anywhere = pl.BlockSpec(memory_space=pl.ANY)
        dma = pltpu.SemaphoreType.DMA
        shape = jax.ShapeDtypeStruct(rhs.shape, F32)
        return pl.pallas_call(
            functools.partial(kernel, n_pts, n_cam, tiles, slots, ct),
            out_shape=(shape, shape),
            in_specs=[vmem] * 4 + [pl.BlockSpec(memory_space=pltpu.SMEM)] + [anywhere] * 4,
            out_specs=(vmem, vmem),
            scratch_shapes=[
                pltpu.VMEM((tiles, 2 * CPAR, slots, LANES), F32),
                pltpu.VMEM((tiles, 6, slots, LANES), F32),
                pltpu.VMEM((3, tiles, LANES), F32),
                pltpu.VMEM((tiles, slots, LANES), jnp.int32),
                pltpu.VMEM((6, tiles, LANES), F32),
                pltpu.VMEM((tiles, slots * CAMS // 2, 2 * LANES), BF16),
                pltpu.VMEM((pairs, width), BF16),
                pltpu.VMEM((rows, 2 * pairs), BF16),
                pltpu.VMEM((pairs, width), F32),
                pltpu.VMEM((2 * pairs, width), BF16),
                pltpu.VMEM((2 * rows, width), BF16),
                pltpu.VMEM((TOG, 160, 2 * LANES), BF16),
                pltpu.VMEM((ITERS, span, 2, 5 * ct, LANES), F32),
                pltpu.VMEM((ITERS, span, 2, 5 * ct, LANES), F32),
                pltpu.VMEM((ITERS, span, 5 * ct, LANES), F32),
                pltpu.VMEM((ITERS, span, 5 * ct, LANES), F32),
                pltpu.VMEM((ITERS, span, 5 * ct, LANES), F32),
                pltpu.VMEM((ITERS + 1, 5 * ct, LANES), F32),
                pltpu.VMEM((ITERS, 5 * ct, LANES), F32),
                pltpu.VMEM((n_cam, 8, LANES), F32),
                pltpu.VMEM((n_pts, 8, LANES), F32),
                dma((4,)),
            ]
            + [dma((ITERS, span))] * 8
            + [dma((n_cam,)), dma((n_cam,)), dma((n_pts,)), dma((n_pts,))],
            compiler_params=pltpu.CompilerParams(
                collective_id=0, has_side_effects=True, vmem_limit_bytes=62_000_000
            ),
        )(
            rhs, damp_cam, precond, jnp.swapaxes(tile_ids, 1, 2), counts,
            jnp.swapaxes(cam_jac, 2, 3), jnp.swapaxes(pt_jac, 2, 3), jnp.swapaxes(damp_pt, 1, 2), cam_index,
        )

    return jax.shard_map(
        on_device,
        mesh=mesh,
        in_specs=(
            P("cam", "pts", None),
            P("cam", "pts", None),
            P("cam", "pts", None),
            P("cam", "pts", None, None, None),
            P("cam", "pts", None, None, None),
            P("cam", "pts", None, None),
            P("cam", "pts", None, None),
            P("cam", "pts", None),
            P("cam", "pts"),
        ),
        out_specs=(P("cam", "pts", None), P("cam", "pts", None)),
        check_vma=False,
    )
```

```python
import functools

import jax
import jax.numpy as jnp
from jax import lax
from jax.experimental import pallas as pl
from jax.experimental.pallas import tpu as pltpu
from jax.sharding import PartitionSpec as P

ITERS = 3
CPAR = 9
CAMS = 64
LANES = 128
SCALE = 0.125
TOG = 12
MESH = pl.DeviceIdType.MESH
F32 = jnp.float32
BF16 = jnp.bfloat16
NT = (((1,), (1,)), ((), ()))
NN = (((1,), (0,)), ((), ()))


def mm(a, b, dims):
    return lax.dot_general(a, b, dims, preferred_element_type=F32)


def split_two(x):
    hi = x.astype(BF16)
    return hi, (x - hi.astype(F32)).astype(BF16)


def kernel(
    n_pts, n_cam, tiles, slots, ct,
    rhs_ref, damp_ref, precond_ref, ids_ref, counts_ref,
    cam_jac_ref, pt_jac_ref, damp_pt_ref, cam_index_ref,
    sol_ref, res_ref,
    jac, pjac, dpt, cidx, inv, sel, pick_hot, sum_hot, picked, spread, win_split, found, given_split,
    win, acc, got, mixed, parts, vecs, bases, scal_cam, scal_pts,
    in_sem, wsend, wrecv, fsend, frecv, psend, precv, rsend, rrecv, csend, crecv, osend, orecv,
):
    half = n_pts // 2
    chips = half * n_cam
    reach = half // 2
    span = 2 * reach + 1
    rows = span * 2 * ct
    width = 5 * LANES
    used = CPAR * CAMS * ct // LANES
    pairs = tiles * slots
    d = lax.axis_index("pts")
    g = lax.axis_index("cam")
    core = lax.rem(d, 2)
    other = 1 - core
    chip = g * half + d // 2

    def at_offset(offset):
        place = lax.rem(chip + (offset + chips), chips)
        return {"pts": lax.rem(place, half) * 2 + core, "cam": place // half}

    twin = {"pts": d + 1 - 2 * core, "cam": g}
    offsets = []
    for far in range(reach, 0, -1):
        offsets += [far, -far]
    places = {offset: at_offset(offset) for offset in offsets}

    loads = [
        pltpu.make_async_copy(pt_jac_ref.at[0], pjac, in_sem.at[0]),
        pltpu.make_async_copy(damp_pt_ref.at[0], dpt, in_sem.at[1]),
        pltpu.make_async_copy(cam_index_ref.at[0], cidx.at[pl.ds(0, tiles)], in_sem.at[2]),
        pltpu.make_async_copy(cam_jac_ref.at[0], jac, in_sem.at[3]),
    ]
    for load in loads:
        load.start()

    barrier = pltpu.get_barrier_semaphore()

    def greet(device):
        pl.semaphore_signal(barrier, inc=1, device_id=device, device_id_type=MESH)

    for offset in offsets:
        greet(places[offset])
    for i in range(1, n_cam):
        greet({"pts": d, "cam": lax.rem(g + i, n_cam)})
    for i in range(1, n_pts):
        greet({"pts": lax.rem(d + i, n_pts), "cam": g})
    pl.semaphore_wait(barrier, len(offsets) + (n_cam - 1) + (n_pts - 1))

    tail = []

    def send(src, dst, ssem, rsem, device):
        copy = pltpu.make_async_remote_copy(
            src_ref=src, dst_ref=dst, send_sem=ssem, recv_sem=rsem, device_id=device, device_id_type=MESH
        )
        copy.start()
        tail.append(copy)
        return copy

    def drain(keep):
        waiting = [copy for copy in tail if all(copy is not kept for kept in keep)]
        tail[:] = keep
        for copy in waiting:
            copy.wait_send()

    def block(ref, *index):
        return ref.at[(*index, pl.ds(0, used))]

    def start_gather(p, value):
        win[p, reach, core] = value
        own = block(win, p, reach, core)
        copies = []
        for offset in offsets:
            slot = reach - offset
            copies.append(send(own, block(win, p, slot, core), wsend.at[p, slot], wrecv.at[p, slot], places[offset]))
        copies.append(send(own, own, fsend.at[p, reach], frecv.at[p, reach], twin))
        return copies

    def finish_gather(p, copies):
        forwards = [copies.pop()]
        drain(copies + forwards)
        for offset, copy in reversed(list(zip(offsets, copies))):
            copy.wait_recv()
            slot = reach - offset
            here = block(win, p, slot, core)
            forwards.append(send(here, here, fsend.at[p, slot], frecv.at[p, slot], twin))
        for copy in forwards:
            copy.wait_recv()

    def reduce_blocks(p, keep):
        swaps = []
        order = offsets + [0]
        for offset in order:
            b = reach + offset
            swaps.append(send(block(acc, p, b, other), block(got, p, b), psend.at[p, b], precv.at[p, b], twin))
        drain(swaps + keep)
        copies = []
        for offset, swap in zip(order, swaps):
            b = reach + offset
            swap.wait_recv()
            total = acc[p, b, core] + got[p, b]
            if offset:
                mixed[p, b] = total
                copies.append(
                    send(block(mixed, p, b), block(parts, p, b), rsend.at[p, b], rrecv.at[p, b], places[offset])
                )
        for offset, copy in zip(offsets, copies):
            copy.wait_recv()
            total = total + parts[p, reach + offset]
        return jnp.where(filled, total, 0.0)

    sub = lax.broadcasted_iota(jnp.int32, (slots, LANES), 0)
    lane = lax.broadcasted_iota(jnp.int32, (slots, LANES), 1)
    low = lane < CAMS
    early = lax.rem(sub, 4) < 2
    aligned = early == low
    top = sub < 4
    filled = lax.broadcasted_iota(jnp.int32, (5 * ct, LANES), 0) < used

    def pack_last(x):
        return jnp.where(low, x, pltpu.roll(pltpu.roll(x, 4, 0), CAMS, 1))

    def unpack_last(x):
        return jnp.where(top, x, pltpu.roll(pltpu.roll(x, 4, 0), CAMS, 1))

    def packed(value):
        groups = [value[:, n * LANES : (n + 1) * LANES] for n in range(4)]
        ending = jnp.concatenate([value[:, 4 * LANES :], jnp.zeros((ct, CAMS), F32)], axis=1)
        return jnp.concatenate(groups + [jnp.where(top, pack_last(ending), 0.0)], axis=0)

    def unpacked(value):
        groups = [value[n * ct : (n + 1) * ct] for n in range(4)]
        return jnp.concatenate(groups + [unpack_last(value[4 * ct :])[:, :CAMS]], axis=1)

    rhs = packed(rhs_ref[0])
    damp = packed(damp_ref[0])
    precond = packed(precond_ref[0])
    vecs[0] = rhs
    scaled = precond * rhs
    bases[0] = scaled
    copies = start_gather(0, scaled)

    shift = (d // 2) * (2 * ct)
    spot = lax.broadcasted_iota(jnp.int32, (slots, width), 1)
    spot = jnp.where(spot < rows, spot, spot - rows)
    ids = jnp.concatenate([ids_ref[0] - shift, jnp.zeros((slots, LANES - tiles), jnp.int32)], axis=1)

    def pick_rows(i, carry):
        hots = []
        for u in range(2):
            own = jnp.take_along_axis(ids, jnp.full_like(ids, 2 * i + u), axis=1, mode="promise_in_bounds")
            hots.append(jnp.where(spot == own[:, :1], 1.0, 0.0))
        pick_hot[pl.ds(pl.multiple_of(i * 16, 16), 16), :] = jnp.concatenate(hots, axis=0).astype(BF16)
        return carry

    lax.fori_loop(0, pairs // 16, pick_rows, 0)
    for i in range(pairs // LANES):
        hot = pick_hot[pl.ds(i * LANES, LANES), pl.ds(0, 3 * LANES)].astype(F32)
        hot = jnp.transpose(hot)[:rows].astype(BF16)
        sum_hot[:, pl.ds(i * LANES, LANES)] = hot
        sum_hot[:, pl.ds(pairs + i * LANES, LANES)] = hot
    loads[0].wait()
    loads[1].wait()
    loads[2].wait()
    loads[3].wait()
    def live_of(t):
        return sub < counts_ref[0, t]

    def point_rows(t):
        return [pjac[t, r] for r in range(6)]

    camera = lax.broadcasted_iota(jnp.int32, (CAMS, LANES), 0)

    def prepare(i, carry):
        sums = [[] for _ in range(6)]
        for u in range(8):
            t = i * 8 + u
            live = live_of(t)
            p = [jnp.where(live, row, 0.0) for row in point_rows(t)]
            for r in range(2 * CPAR):
                jac[t, r] = jnp.where(live, jac[t, r], 0.0)
            for n, (a, b) in enumerate(((0, 0), (0, 1), (0, 2), (1, 1), (1, 2), (2, 2))):
                sums[n].append(jnp.sum(p[a] * p[b] + p[3 + a] * p[3 + b], axis=0, keepdims=True))
            for k in range(slots):
                index = cidx[t, pl.ds(k, 1), :]
                hot = jnp.where(camera == index, 1.0, 0.0).astype(BF16)
                sel[TOG + t, pl.ds((k // 2) * CAMS, CAMS), pl.ds((k % 2) * LANES, LANES)] = hot
        here = pl.ds(pl.multiple_of(i * 8, 8), 8)
        v00, v01, v02, v11, v12, v22 = [jnp.concatenate(part, axis=0) for part in sums]
        v00 = v00 + dpt[0, here, :]
        v11 = v11 + dpt[1, here, :]
        v22 = v22 + dpt[2, here, :]
        c00 = v11 * v22 - v12 * v12
        c01 = v12 * v02 - v01 * v22
        c02 = v01 * v12 - v11 * v02
        c11 = v22 * v00 - v02 * v02
        c12 = v02 * v01 - v00 * v12
        c22 = v00 * v11 - v01 * v01
        det = v00 * c00 + v01 * c01 + v02 * c02
        for n, value in enumerate((c00, c01, c02, c11, c12, c22)):
            inv[n, here, :] = value / det
        return carry

    lax.fori_loop(0, tiles // 8, prepare, 0)

    together = TOG
    lower = 80
    parity = lax.rem(lax.broadcasted_iota(jnp.int32, (CPAR * slots, LANES), 0), 2)
    odd_rows = parity.astype(F32).astype(BF16)
    even_rows = (1 - parity).astype(F32).astype(BF16)
    for u in range(together):
        cidx[tiles + u] = jnp.zeros((slots, LANES), jnp.int32)
        given_split[u] = jnp.zeros((2 * lower, 2 * LANES), BF16)

    def look_up(t, u):
        index = cidx[t]
        for first in range(2):
            for j in range(first, CPAR, 2):
                table = picked[pl.ds(t * slots, slots), pl.ds((j // 2) * LANES, LANES)]
                found[u, j] = jnp.take_along_axis(table, index + CAMS * first, axis=1, mode="promise_in_bounds")

    def observe(t, u):
        j_rows = [jac[t, r] for r in range(2 * CPAR)]
        p = point_rows(t)
        q = []
        for r in range(2):
            total = j_rows[CPAR * r] * found[u, 0]
            for j in range(1, CPAR):
                total = total + j_rows[CPAR * r + j] * found[u, j]
            q.append(total)
        y = [jnp.sum(p[a] * q[0] + p[3 + a] * q[1], axis=0, keepdims=True) for a in range(3)]
        m = [inv[n, pl.ds(t, 1), :] for n in range(6)]
        z = [
            m[0] * y[0] + m[1] * y[1] + m[2] * y[2],
            m[1] * y[0] + m[3] * y[1] + m[4] * y[2],
            m[2] * y[0] + m[4] * y[1] + m[5] * y[2],
        ]
        e = []
        for r in range(2):
            back = p[3 * r] * z[0] + p[3 * r + 1] * z[1] + p[3 * r + 2] * z[2]
            e.append(q[r] - back)
        given = jnp.concatenate([j_rows[j] * e[0] + j_rows[CPAR + j] * e[1] for j in range(CPAR)], axis=0)
        hi, lo = split_two(given)
        heights = CPAR * slots
        given_split[u, pl.ds(0, heights), :] = jnp.concatenate([hi * even_rows, hi * odd_rows], axis=1)
        given_split[u, pl.ds(lower, heights), :] = jnp.concatenate([lo * even_rows, lo * odd_rows], axis=1)
        return q[0] * e[0] + q[1] * e[1]

    def camera_sums(t, u):
        out = mm(given_split[u], sel[t], NT)

        def diagonal(j):
            both = []
            for n in range(slots // 4):
                cut = slice(n * LANES, (n + 1) * LANES)
                both.append(
                    out[j * slots : (j + 1) * slots, cut] + out[lower + j * slots : lower + (j + 1) * slots, cut]
                )
            return jnp.where(top, both[0], both[1])

        merged = []
        for i in range(0, CPAR, 2):
            first = diagonal(i)
            second = diagonal(i + 1) if i + 1 < CPAR else jnp.zeros_like(first)
            turned = pltpu.roll(jnp.where(early, second, first), CAMS, 1)
            merged.append(jnp.where(aligned, jnp.where(early, first, second), turned))
        return jnp.concatenate(merged, axis=1)

    steps = tiles // together

    def look_step(i):
        for u in range(together):
            look_up(i * together + u, u)

    def observe_step(i, bend):
        for u in range(together):
            bend = bend + observe(i * together + u, u)
        return bend

    def sum_step(i):
        terms = [camera_sums(i * together + u, u) for u in range(together)]
        for u in range(0, together, 2):
            hi, lo = split_two(jnp.concatenate(terms[u : u + 2], axis=0))
            start = pl.multiple_of((i * together + u) * slots, 16)
            spread[0, pl.ds(start, 16), :] = hi
            spread[1, pl.ds(start, 16), :] = lo

    def all_steps(i, bend):
        sum_step(i)
        bend = observe_step(i, bend)
        look_step(i + 1)
        return bend

    wanted = [(i, j) for j in range(ITERS) for i in range(j + 1)]

    def lane_sums(product):
        line = product[:ct]
        for n in range(1, 5):
            line = line + product[n * ct : (n + 1) * ct]
        return line

    def start_sums(bend):
        lines = [lane_sums(bases[i] * vecs[j]) for i, j in wanted]
        last = bases[ITERS - 1]
        lines.append(SCALE * (bend + lane_sums(damp * last * last)))
        lines = [jnp.sum(line, axis=0, keepdims=True) for line in lines]
        lines.append(jnp.zeros((8 - len(lines), LANES), F32))
        scal_cam[g] = jnp.concatenate(lines, axis=0)
        return [
            send(scal_cam.at[g], scal_cam.at[g], csend.at[i], crecv.at[i], {"pts": d, "cam": lax.rem(g + i, n_cam)})
            for i in range(1, n_cam)
        ]

    def cross_sums(copies):
        for copy in copies:
            copy.wait_recv()
        total = scal_cam[0]
        for i in range(1, n_cam):
            total = total + scal_cam[i]
        scal_pts[d] = total
        return [
            send(scal_pts.at[d], scal_pts.at[d], osend.at[i], orecv.at[i], {"pts": lax.rem(d + i, n_pts), "cam": g})
            for i in range(1, n_pts)
        ]

    for p in range(ITERS):
        finish_gather(p, copies)
        for n in range(5):
            window = win[p, :, :, pl.ds(n * ct, ct), :].reshape(rows, LANES)
            if n == 4:
                window = jnp.concatenate(
                    [unpack_last(window[i * ct : (i + 1) * ct]) for i in range(2 * span)], axis=0
                )
            hi, lo = split_two(window)
            cut = pl.ds(n * LANES, LANES)
            win_split[pl.ds(0, rows), cut] = hi
            win_split[pl.ds(rows, rows), cut] = lo

        def pick(i, carry):
            here = pl.ds(pl.multiple_of(i * (pairs // 2), 16), pairs // 2)
            picked[here, :] = mm(pick_hot[here, pl.ds(0, 2 * rows)], win_split[...], NN)
            return carry

        lax.fori_loop(0, 2, pick, 0)
        look_step(0)
        bend = lax.fori_loop(0, steps, all_steps, jnp.zeros((slots, LANES), F32))
        sum_step(steps)
        if p + 1 == ITERS:
            started = start_sums(bend)
        for low_group, high_group in ((0, 2), (2, 4), (4, 5)):
            cut = pl.ds(low_group * LANES, (high_group - low_group) * LANES)
            given = jnp.concatenate([spread[n, pl.ds(TOG * slots, pairs), cut] for n in range(2)], axis=0)
            sums = mm(sum_hot[...], given, NN)
            for i in range(low_group, high_group):
                value = sums[:, (i - low_group) * LANES : (i - low_group + 1) * LANES]
                if i == 4:
                    value = jnp.concatenate(
                        [pack_last(value[n * ct : (n + 1) * ct]) for n in range(2 * span)], axis=0
                    )
                acc[p, :, :, pl.ds(i * ct, ct), :] = value.reshape(span, 2, ct, LANES)
        if p + 1 == ITERS:
            started = cross_sums(started)
        total = reduce_blocks(p, started if p + 1 == ITERS else [])
        mapped = SCALE * (total + damp * bases[p])
        vecs[p + 1] = mapped
        if p + 1 < ITERS:
            scaled = precond * mapped
            bases[p + 1] = scaled
            copies = start_gather(p + 1, scaled)

    for copy in started:
        copy.wait_recv()
    total = scal_pts[0]
    for i in range(1, n_pts):
        total = total + scal_pts[i]
    sums = jnp.broadcast_to(jnp.sum(total, axis=1, keepdims=True), (8, LANES))
    gram = {}
    for i, (a, b) in enumerate(wanted):
        gram[a, b] = gram[b, a] = sums[i : i + 1, :]
    for i in range(ITERS - 1):
        gram[i, ITERS] = gram[i + 1, ITERS - 1]
    gram[ITERS - 1, ITERS] = sums[len(wanted) : len(wanted) + 1, :]

    one = jnp.ones((1, LANES), F32)
    nil = jnp.zeros((1, LANES), F32)
    x = [nil] * ITERS
    r = [one] + [nil] * ITERS
    s = [one] + [nil] * (ITERS - 1)
    energy = gram[0, 0]
    for p in range(ITERS):
        mapped = [nil] + [value * (1.0 / SCALE) for value in s]
        steep = nil
        for i in range(p + 1):
            row = nil
            for j in range(1, p + 2):
                row = row + mapped[j] * gram[i, j]
            steep = steep + s[i] * row
        step = energy / steep
        x = [a + step * b for a, b in zip(x, s)]
        r = [a - step * b for a, b in zip(r, mapped)]
        if p + 1 < ITERS:
            following = nil
            for i in range(p + 2):
                row = nil
                for j in range(p + 2):
                    row = row + r[j] * gram[i, j]
                following = following + r[i] * row
            ratio = following / energy
            s = [a + ratio * b for a, b in zip(r[:ITERS], s)]
            energy = following

    def spread_out(value):
        return jnp.broadcast_to(value, (5 * ct, LANES))

    solution_value = spread_out(x[0]) * bases[0]
    residual_value = spread_out(r[0]) * vecs[0]
    for i in range(1, ITERS):
        solution_value = solution_value + spread_out(x[i]) * bases[i]
    for i in range(1, ITERS + 1):
        residual_value = residual_value + spread_out(r[i]) * vecs[i]
    drain([])
    sol_ref[0] = unpacked(solution_value)
    res_ref[0] = unpacked(residual_value)


def solution(mesh):
    n_pts, n_cam = mesh.shape["pts"], mesh.shape["cam"]

    def on_device(rhs, damp_cam, precond, cam_jac, pt_jac, damp_pt, cam_index, tile_ids, counts):
        ct = rhs.shape[1]
        tiles, slots = cam_jac.shape[1:3]
        pairs = tiles * slots
        span = n_pts // 2 + 1
        rows = span * 2 * ct
        width = 5 * LANES
        vmem = pl.BlockSpec(memory_space=pltpu.VMEM)
        anywhere = pl.BlockSpec(memory_space=pl.ANY)
        dma = pltpu.SemaphoreType.DMA
        shape = jax.ShapeDtypeStruct(rhs.shape, F32)
        return pl.pallas_call(
            functools.partial(kernel, n_pts, n_cam, tiles, slots, ct),
            out_shape=(shape, shape),
            in_specs=[vmem] * 4 + [pl.BlockSpec(memory_space=pltpu.SMEM)] + [anywhere] * 4,
            out_specs=(vmem, vmem),
            scratch_shapes=[
                pltpu.VMEM((tiles, 2 * CPAR, slots, LANES), F32),
                pltpu.VMEM((tiles, 6, slots, LANES), F32),
                pltpu.VMEM((3, tiles, LANES), F32),
                pltpu.VMEM((tiles + TOG, slots, LANES), jnp.int32),
                pltpu.VMEM((6, tiles, LANES), F32),
                pltpu.VMEM((TOG + tiles, slots * CAMS // 2, 2 * LANES), BF16),
                pltpu.VMEM((pairs, width), BF16),
                pltpu.VMEM((rows, 2 * pairs), BF16),
                pltpu.VMEM((pairs + TOG * slots, width), F32),
                pltpu.VMEM((2, TOG * slots + pairs, width), BF16),
                pltpu.VMEM((2 * rows, width), BF16),
                pltpu.VMEM((TOG, CPAR, slots, LANES), F32),
                pltpu.VMEM((TOG, 160, 2 * LANES), BF16),
                pltpu.VMEM((ITERS, span, 2, 5 * ct, LANES), F32),
                pltpu.VMEM((ITERS, span, 2, 5 * ct, LANES), F32),
                pltpu.VMEM((ITERS, span, 5 * ct, LANES), F32),
                pltpu.VMEM((ITERS, span, 5 * ct, LANES), F32),
                pltpu.VMEM((ITERS, span, 5 * ct, LANES), F32),
                pltpu.VMEM((ITERS + 1, 5 * ct, LANES), F32),
                pltpu.VMEM((ITERS, 5 * ct, LANES), F32),
                pltpu.VMEM((n_cam, 8, LANES), F32),
                pltpu.VMEM((n_pts, 8, LANES), F32),
                dma((4,)),
            ]
            + [dma((ITERS, span))] * 8
            + [dma((n_cam,)), dma((n_cam,)), dma((n_pts,)), dma((n_pts,))],
            compiler_params=pltpu.CompilerParams(
                collective_id=0, has_side_effects=True, vmem_limit_bytes=62_000_000
            ),
        )(
            rhs, damp_cam, precond, jnp.swapaxes(tile_ids, 1, 2), counts,
            jnp.swapaxes(cam_jac, 2, 3), jnp.swapaxes(pt_jac, 2, 3), jnp.swapaxes(damp_pt, 1, 2), cam_index,
        )

    return jax.shard_map(
        on_device,
        mesh=mesh,
        in_specs=(
            P("cam", "pts", None),
            P("cam", "pts", None),
            P("cam", "pts", None),
            P("cam", "pts", None, None, None),
            P("cam", "pts", None, None, None),
            P("cam", "pts", None, None),
            P("cam", "pts", None, None),
            P("cam", "pts", None),
            P("cam", "pts"),
        ),
        out_specs=(P("cam", "pts", None), P("cam", "pts", None)),
        check_vma=False,
    )
```

```python
import functools

import jax
import jax.numpy as jnp
from jax import lax
from jax.experimental import pallas as pl
from jax.experimental.pallas import tpu as pltpu
from jax.sharding import PartitionSpec as P

ITERS = 3
CPAR = 9
CAMS = 64
LANES = 128
SCALE = 0.125
TOG = 12
MESH = pl.DeviceIdType.MESH
F32 = jnp.float32
BF16 = jnp.bfloat16
NT = (((1,), (1,)), ((), ()))
NN = (((1,), (0,)), ((), ()))


def mm(a, b, dims):
    return lax.dot_general(a, b, dims, preferred_element_type=F32)


def split_two(x):
    hi = x.astype(BF16)
    return hi, (x - hi.astype(F32)).astype(BF16)


def kernel(
    n_pts, n_cam, tiles, slots, ct,
    rhs_ref, damp_ref, precond_ref, ids_ref, counts_ref,
    cam_jac_ref, pt_jac_ref, damp_pt_ref, cam_index_ref,
    out_ref,
    jac, pjac, dpt, cidx, inv, sel, pick_hot, sum_hot, picked, spread, win_split, found, given_split,
    win, acc, got, mixed, parts, vecs, bases, scal_cam, scal_pts,
    in_sem, wsend, wrecv, fsend, frecv, psend, precv, rsend, rrecv, csend, crecv, osend, orecv,
):
    half = n_pts // 2
    chips = half * n_cam
    reach = half // 2
    span = 2 * reach + 1
    rows = span * 2 * ct
    width = 5 * LANES
    used = CPAR * CAMS * ct // LANES
    pairs = tiles * slots
    d = lax.axis_index("pts")
    g = lax.axis_index("cam")
    core = lax.rem(d, 2)
    other = 1 - core
    chip = g * half + d // 2

    def at_offset(offset):
        place = lax.rem(chip + (offset + chips), chips)
        return {"pts": lax.rem(place, half) * 2 + core, "cam": place // half}

    twin = {"pts": d + 1 - 2 * core, "cam": g}
    offsets = []
    for far in range(reach, 0, -1):
        offsets += [far, -far]
    places = {offset: at_offset(offset) for offset in offsets}

    loads = [
        pltpu.make_async_copy(pt_jac_ref.at[0], pjac, in_sem.at[0]),
        pltpu.make_async_copy(damp_pt_ref.at[0], dpt, in_sem.at[1]),
        pltpu.make_async_copy(cam_index_ref.at[0], cidx.at[pl.ds(0, tiles)], in_sem.at[2]),
        pltpu.make_async_copy(cam_jac_ref.at[0], jac, in_sem.at[3]),
    ]
    for load in loads:
        load.start()

    barrier = pltpu.get_barrier_semaphore()

    def greet(device):
        pl.semaphore_signal(barrier, inc=1, device_id=device, device_id_type=MESH)

    for offset in offsets:
        greet(places[offset])
    for i in range(1, n_cam):
        greet({"pts": d, "cam": lax.rem(g + i, n_cam)})
    for i in range(1, n_pts):
        greet({"pts": lax.rem(d + i, n_pts), "cam": g})

    tail = []

    def send(src, dst, ssem, rsem, device):
        copy = pltpu.make_async_remote_copy(
            src_ref=src, dst_ref=dst, send_sem=ssem, recv_sem=rsem, device_id=device, device_id_type=MESH
        )
        copy.start()
        tail.append(copy)
        return copy

    def drain(keep):
        waiting = [copy for copy in tail if all(copy is not kept for kept in keep)]
        tail[:] = keep
        for copy in waiting:
            copy.wait_send()

    def block(ref, *index):
        return ref.at[(*index, pl.ds(0, used))]

    def start_gather(p, value):
        win[p, reach, core] = value
        own = block(win, p, reach, core)
        copies = []
        for offset in offsets:
            slot = reach - offset
            copies.append(send(own, block(win, p, slot, core), wsend.at[p, slot], wrecv.at[p, slot], places[offset]))
        copies.append(send(own, own, fsend.at[p, reach], frecv.at[p, reach], twin))
        return copies

    def finish_gather(p, copies):
        forwards = [copies.pop()]
        drain(copies + forwards)
        for offset, copy in list(zip(offsets, copies)):
            copy.wait_recv()
            slot = reach - offset
            here = block(win, p, slot, core)
            forwards.append(send(here, here, fsend.at[p, slot], frecv.at[p, slot], twin))
        for copy in forwards:
            copy.wait_recv()

    def reduce_blocks(p, keep, meanwhile):
        swaps = []
        order = offsets + [0]
        for offset in order:
            b = reach + offset
            swaps.append(send(block(acc, p, b, other), block(got, p, b), psend.at[p, b], precv.at[p, b], twin))
        drain(swaps + keep)
        copies = []
        for offset, swap in zip(order, swaps):
            b = reach + offset
            swap.wait_recv()
            total = acc[p, b, core] + got[p, b]
            if offset:
                mixed[p, b] = total
                copies.append(
                    send(block(mixed, p, b), block(parts, p, b), rsend.at[p, b], rrecv.at[p, b], places[offset])
                )
        meanwhile()
        for offset, copy in zip(offsets, copies):
            copy.wait_recv()
            total = total + parts[p, reach + offset]
        return jnp.where(filled, total, 0.0)

    sub = lax.broadcasted_iota(jnp.int32, (slots, LANES), 0)
    lane = lax.broadcasted_iota(jnp.int32, (slots, LANES), 1)
    low = lane < CAMS
    early = lax.rem(sub, 4) < 2
    aligned = early == low
    top = sub < 4
    filled = lax.broadcasted_iota(jnp.int32, (5 * ct, LANES), 0) < used

    def pack_last(x):
        return jnp.where(low, x, pltpu.roll(pltpu.roll(x, 4, 0), CAMS, 1))

    def unpack_last(x):
        return jnp.where(top, x, pltpu.roll(pltpu.roll(x, 4, 0), CAMS, 1))

    def packed(value):
        groups = [value[:, n * LANES : (n + 1) * LANES] for n in range(4)]
        ending = jnp.concatenate([value[:, 4 * LANES :], jnp.zeros((ct, CAMS), F32)], axis=1)
        return jnp.concatenate(groups + [jnp.where(top, pack_last(ending), 0.0)], axis=0)

    def unpacked(value):
        groups = [value[n * ct : (n + 1) * ct] for n in range(4)]
        return jnp.concatenate(groups + [unpack_last(value[4 * ct :])[:, :CAMS]], axis=1)

    rhs = packed(rhs_ref[0])
    damp = packed(damp_ref[0])
    precond = packed(precond_ref[0])
    shift = (d // 2) * (2 * ct)
    spot = lax.broadcasted_iota(jnp.int32, (slots, width), 1)
    spot = jnp.where(spot < rows, spot, spot - rows)
    ids = jnp.concatenate([ids_ref[0] - shift, jnp.zeros((slots, LANES - tiles), jnp.int32)], axis=1)

    def pick_rows(i, carry):
        hots = []
        for u in range(2):
            own = jnp.take_along_axis(ids, jnp.full_like(ids, 2 * i + u), axis=1, mode="promise_in_bounds")
            hots.append(jnp.where(spot == own[:, :1], 1.0, 0.0))
        pick_hot[pl.ds(pl.multiple_of(i * 16, 16), 16), :] = jnp.concatenate(hots, axis=0).astype(BF16)
        return carry

    lax.fori_loop(0, pairs // 16, pick_rows, 0)
    for i in range(pairs // LANES):
        hot = pick_hot[pl.ds(i * LANES, LANES), pl.ds(0, 3 * LANES)].astype(F32)
        hot = jnp.transpose(hot)[:rows].astype(BF16)
        sum_hot[:, pl.ds(i * LANES, LANES)] = hot
        sum_hot[:, pl.ds(pairs + i * LANES, LANES)] = hot
    pl.semaphore_wait(barrier, len(offsets) + (n_cam - 1) + (n_pts - 1))
    vecs[0] = rhs
    scaled = precond * rhs
    bases[0] = scaled
    copies = start_gather(0, scaled)

    loads[0].wait()
    loads[1].wait()
    loads[2].wait()
    loads[3].wait()
    def live_of(t):
        return sub < counts_ref[0, t]

    def point_rows(t):
        return [pjac[t, r] for r in range(6)]

    camera = lax.broadcasted_iota(jnp.int32, (CAMS, LANES), 0)

    def prepare(i, carry):
        sums = [[] for _ in range(6)]
        for u in range(8):
            t = i * 8 + u
            live = live_of(t)
            p = [jnp.where(live, row, 0.0) for row in point_rows(t)]
            for r in range(2 * CPAR):
                jac[t, r] = jnp.where(live, jac[t, r], 0.0)
            for n, (a, b) in enumerate(((0, 0), (0, 1), (0, 2), (1, 1), (1, 2), (2, 2))):
                sums[n].append(jnp.sum(p[a] * p[b] + p[3 + a] * p[3 + b], axis=0, keepdims=True))
            for k in range(slots):
                index = cidx[t, pl.ds(k, 1), :]
                hot = jnp.where(camera == index, 1.0, 0.0).astype(BF16)
                sel[TOG + t, pl.ds((k // 2) * CAMS, CAMS), pl.ds((k % 2) * LANES, LANES)] = hot
        here = pl.ds(pl.multiple_of(i * 8, 8), 8)
        v00, v01, v02, v11, v12, v22 = [jnp.concatenate(part, axis=0) for part in sums]
        v00 = v00 + dpt[0, here, :]
        v11 = v11 + dpt[1, here, :]
        v22 = v22 + dpt[2, here, :]
        c00 = v11 * v22 - v12 * v12
        c01 = v12 * v02 - v01 * v22
        c02 = v01 * v12 - v11 * v02
        c11 = v22 * v00 - v02 * v02
        c12 = v02 * v01 - v00 * v12
        c22 = v00 * v11 - v01 * v01
        det = v00 * c00 + v01 * c01 + v02 * c02
        for n, value in enumerate((c00, c01, c02, c11, c12, c22)):
            inv[n, here, :] = value / det
        return carry

    lax.fori_loop(0, tiles // 8, prepare, 0)

    together = TOG
    lower = 80
    parity = lax.rem(lax.broadcasted_iota(jnp.int32, (CPAR * slots, LANES), 0), 2)
    odd_rows = parity.astype(F32).astype(BF16)
    even_rows = (1 - parity).astype(F32).astype(BF16)
    for u in range(together):
        cidx[tiles + u] = jnp.zeros((slots, LANES), jnp.int32)
        given_split[u] = jnp.zeros((2 * lower, 2 * LANES), BF16)

    def look_up(t, u):
        index = cidx[t]
        for first in range(2):
            for j in range(first, CPAR, 2):
                table = picked[pl.ds(t * slots, slots), pl.ds((j // 2) * LANES, LANES)]
                found[u, j] = jnp.take_along_axis(table, index + CAMS * first, axis=1, mode="promise_in_bounds")

    def observe(t, u):
        j_rows = [jac[t, r] for r in range(2 * CPAR)]
        p = point_rows(t)
        q = []
        for r in range(2):
            total = j_rows[CPAR * r] * found[u, 0]
            for j in range(1, CPAR):
                total = total + j_rows[CPAR * r + j] * found[u, j]
            q.append(total)
        y = [jnp.sum(p[a] * q[0] + p[3 + a] * q[1], axis=0, keepdims=True) for a in range(3)]
        m = [inv[n, pl.ds(t, 1), :] for n in range(6)]
        z = [
            m[0] * y[0] + m[1] * y[1] + m[2] * y[2],
            m[1] * y[0] + m[3] * y[1] + m[4] * y[2],
            m[2] * y[0] + m[4] * y[1] + m[5] * y[2],
        ]
        e = []
        for r in range(2):
            back = p[3 * r] * z[0] + p[3 * r + 1] * z[1] + p[3 * r + 2] * z[2]
            e.append(q[r] - back)
        given = jnp.concatenate([j_rows[j] * e[0] + j_rows[CPAR + j] * e[1] for j in range(CPAR)], axis=0)
        hi, lo = split_two(given)
        heights = CPAR * slots
        given_split[u, pl.ds(0, heights), :] = jnp.concatenate([hi * even_rows, hi * odd_rows], axis=1)
        given_split[u, pl.ds(lower, heights), :] = jnp.concatenate([lo * even_rows, lo * odd_rows], axis=1)
        return q[0] * e[0] + q[1] * e[1]

    def camera_sums(t, u):
        out = mm(given_split[u], sel[t], NT)

        def diagonal(j):
            both = []
            for n in range(slots // 4):
                cut = slice(n * LANES, (n + 1) * LANES)
                both.append(
                    out[j * slots : (j + 1) * slots, cut] + out[lower + j * slots : lower + (j + 1) * slots, cut]
                )
            return jnp.where(top, both[0], both[1])

        merged = []
        for i in range(0, CPAR, 2):
            first = diagonal(i)
            second = diagonal(i + 1) if i + 1 < CPAR else jnp.zeros_like(first)
            turned = pltpu.roll(jnp.where(early, second, first), CAMS, 1)
            merged.append(jnp.where(aligned, jnp.where(early, first, second), turned))
        return jnp.concatenate(merged, axis=1)

    steps = tiles // together

    def look_step(i):
        for u in range(together):
            look_up(i * together + u, u)

    def observe_step(i, bend):
        for u in range(together):
            bend = bend + observe(i * together + u, u)
        return bend

    def sum_step(i):
        terms = [camera_sums(i * together + u, u) for u in range(together)]
        for u in range(0, together, 2):
            hi, lo = split_two(jnp.concatenate(terms[u : u + 2], axis=0))
            start = pl.multiple_of((i * together + u) * slots, 16)
            spread[0, pl.ds(start, 16), :] = hi
            spread[1, pl.ds(start, 16), :] = lo

    def all_steps(i, bend):
        sum_step(i)
        bend = observe_step(i, bend)
        look_step(i + 1)
        return bend

    wanted = [(i, j) for j in range(ITERS) for i in range(j + 1)]

    def lane_sums(product):
        line = product[:ct]
        for n in range(1, 5):
            line = line + product[n * ct : (n + 1) * ct]
        return line

    def start_sums(bend):
        lines = [lane_sums(bases[i] * vecs[j]) for i, j in wanted]
        last = bases[ITERS - 1]
        lines.append(SCALE * (bend + lane_sums(damp * last * last)))
        lines = [jnp.sum(line, axis=0, keepdims=True) for line in lines]
        lines.append(jnp.zeros((8 - len(lines), LANES), F32))
        scal_cam[g] = jnp.concatenate(lines, axis=0)
        return [
            send(scal_cam.at[g], scal_cam.at[g], csend.at[i], crecv.at[i], {"pts": d, "cam": lax.rem(g + i, n_cam)})
            for i in range(1, n_cam)
        ]

    def cross_sums(copies):
        for copy in copies:
            copy.wait_recv()
        total = scal_cam[0]
        for i in range(1, n_cam):
            total = total + scal_cam[i]
        scal_pts[d] = total
        return [
            send(scal_pts.at[d], scal_pts.at[d], osend.at[i], orecv.at[i], {"pts": lax.rem(d + i, n_pts), "cam": g})
            for i in range(1, n_pts)
        ]

    for p in range(ITERS):
        finish_gather(p, copies)
        for n in range(5):
            window = win[p, :, :, pl.ds(n * ct, ct), :].reshape(rows, LANES)
            if n == 4:
                window = jnp.concatenate(
                    [unpack_last(window[i * ct : (i + 1) * ct]) for i in range(2 * span)], axis=0
                )
            hi, lo = split_two(window)
            cut = pl.ds(n * LANES, LANES)
            win_split[pl.ds(0, rows), cut] = hi
            win_split[pl.ds(rows, rows), cut] = lo

        def pick(i, carry):
            here = pl.ds(pl.multiple_of(i * (pairs // 2), 16), pairs // 2)
            picked[here, :] = mm(pick_hot[here, pl.ds(0, 2 * rows)], win_split[...], NN)
            return carry

        lax.fori_loop(0, 2, pick, 0)
        look_step(0)
        bend = lax.fori_loop(0, steps, all_steps, jnp.zeros((slots, LANES), F32))
        sum_step(steps)
        if p + 1 == ITERS:
            started = start_sums(bend)
        for low_group, high_group in ((0, 2), (2, 4), (4, 5)):
            cut = pl.ds(low_group * LANES, (high_group - low_group) * LANES)
            given = jnp.concatenate([spread[n, pl.ds(TOG * slots, pairs), cut] for n in range(2)], axis=0)
            sums = mm(sum_hot[...], given, NN)
            for i in range(low_group, high_group):
                value = sums[:, (i - low_group) * LANES : (i - low_group + 1) * LANES]
                if i == 4:
                    value = jnp.concatenate(
                        [pack_last(value[n * ct : (n + 1) * ct]) for n in range(2 * span)], axis=0
                    )
                acc[p, :, :, pl.ds(i * ct, ct), :] = value.reshape(span, 2, ct, LANES)
        crossing = []

        def meanwhile():
            if p + 1 == ITERS:
                crossing.extend(cross_sums(started))

        total = reduce_blocks(p, started if p + 1 == ITERS else [], meanwhile)
        mapped = SCALE * (total + damp * bases[p])
        vecs[p + 1] = mapped
        if p + 1 < ITERS:
            scaled = precond * mapped
            bases[p + 1] = scaled
            copies = start_gather(p + 1, scaled)

    for copy in crossing:
        copy.wait_recv()
    total = scal_pts[0]
    for i in range(1, n_pts):
        total = total + scal_pts[i]
    sums = jnp.broadcast_to(jnp.sum(total, axis=1, keepdims=True), (8, LANES))
    gram = {}
    for i, (a, b) in enumerate(wanted):
        gram[a, b] = gram[b, a] = sums[i : i + 1, :]
    for i in range(ITERS - 1):
        gram[i, ITERS] = gram[i + 1, ITERS - 1]
    gram[ITERS - 1, ITERS] = sums[len(wanted) : len(wanted) + 1, :]

    one = jnp.ones((1, LANES), F32)
    nil = jnp.zeros((1, LANES), F32)
    x = [nil] * ITERS
    r = [one] + [nil] * ITERS
    s = [one] + [nil] * (ITERS - 1)
    energy = gram[0, 0]
    for p in range(ITERS):
        mapped = [nil] + [value * (1.0 / SCALE) for value in s]
        steep = nil
        for i in range(p + 1):
            row = nil
            for j in range(1, p + 2):
                row = row + mapped[j] * gram[i, j]
            steep = steep + s[i] * row
        step = energy / steep
        x = [a + step * b for a, b in zip(x, s)]
        r = [a - step * b for a, b in zip(r, mapped)]
        if p + 1 < ITERS:
            following = nil
            for i in range(p + 2):
                row = nil
                for j in range(p + 2):
                    row = row + r[j] * gram[i, j]
                following = following + r[i] * row
            ratio = following / energy
            s = [a + ratio * b for a, b in zip(r[:ITERS], s)]
            energy = following

    def spread_out(value):
        return jnp.broadcast_to(value, (5 * ct, LANES))

    solution_value = spread_out(x[0]) * bases[0]
    residual_value = spread_out(r[0]) * vecs[0]
    for i in range(1, ITERS):
        solution_value = solution_value + spread_out(x[i]) * bases[i]
    for i in range(1, ITERS + 1):
        residual_value = residual_value + spread_out(r[i]) * vecs[i]
    drain([])
    out_ref[0] = unpacked(solution_value)
    out_ref[1] = unpacked(residual_value)


def solution(mesh):
    n_pts, n_cam = mesh.shape["pts"], mesh.shape["cam"]

    def on_device(rhs, damp_cam, precond, cam_jac, pt_jac, damp_pt, cam_index, tile_ids, counts):
        ct = rhs.shape[1]
        tiles, slots = cam_jac.shape[1:3]
        pairs = tiles * slots
        span = n_pts // 2 + 1
        rows = span * 2 * ct
        width = 5 * LANES
        vmem = pl.BlockSpec(memory_space=pltpu.VMEM)
        anywhere = pl.BlockSpec(memory_space=pl.ANY)
        dma = pltpu.SemaphoreType.DMA
        both = pl.pallas_call(
            functools.partial(kernel, n_pts, n_cam, tiles, slots, ct),
            out_shape=jax.ShapeDtypeStruct((2, *rhs.shape[1:]), F32),
            in_specs=[vmem] * 4 + [pl.BlockSpec(memory_space=pltpu.SMEM)] + [anywhere] * 4,
            out_specs=vmem,
            scratch_shapes=[
                pltpu.VMEM((tiles, 2 * CPAR, slots, LANES), F32),
                pltpu.VMEM((tiles, 6, slots, LANES), F32),
                pltpu.VMEM((3, tiles, LANES), F32),
                pltpu.VMEM((tiles + TOG, slots, LANES), jnp.int32),
                pltpu.VMEM((6, tiles, LANES), F32),
                pltpu.VMEM((TOG + tiles, slots * CAMS // 2, 2 * LANES), BF16),
                pltpu.VMEM((pairs, width), BF16),
                pltpu.VMEM((rows, 2 * pairs), BF16),
                pltpu.VMEM((pairs + TOG * slots, width), F32),
                pltpu.VMEM((2, TOG * slots + pairs, width), BF16),
                pltpu.VMEM((2 * rows, width), BF16),
                pltpu.VMEM((TOG, CPAR, slots, LANES), F32),
                pltpu.VMEM((TOG, 160, 2 * LANES), BF16),
                pltpu.VMEM((ITERS, span, 2, 5 * ct, LANES), F32),
                pltpu.VMEM((ITERS, span, 2, 5 * ct, LANES), F32),
                pltpu.VMEM((ITERS, span, 5 * ct, LANES), F32),
                pltpu.VMEM((ITERS, span, 5 * ct, LANES), F32),
                pltpu.VMEM((ITERS, span, 5 * ct, LANES), F32),
                pltpu.VMEM((ITERS + 1, 5 * ct, LANES), F32),
                pltpu.VMEM((ITERS, 5 * ct, LANES), F32),
                pltpu.VMEM((n_cam, 8, LANES), F32),
                pltpu.VMEM((n_pts, 8, LANES), F32),
                dma((4,)),
            ]
            + [dma((ITERS, span))] * 8
            + [dma((n_cam,)), dma((n_cam,)), dma((n_pts,)), dma((n_pts,))],
            compiler_params=pltpu.CompilerParams(
                collective_id=0, has_side_effects=True, vmem_limit_bytes=62_000_000
            ),
        )(
            rhs, damp_cam, precond, jnp.swapaxes(tile_ids, 1, 2), counts,
            jnp.swapaxes(cam_jac, 2, 3), jnp.swapaxes(pt_jac, 2, 3), jnp.swapaxes(damp_pt, 1, 2), cam_index,
        )
        return both[:1], both[1:]

    return jax.shard_map(
        on_device,
        mesh=mesh,
        in_specs=(
            P("cam", "pts", None),
            P("cam", "pts", None),
            P("cam", "pts", None),
            P("cam", "pts", None, None, None),
            P("cam", "pts", None, None, None),
            P("cam", "pts", None, None),
            P("cam", "pts", None, None),
            P("cam", "pts", None),
            P("cam", "pts"),
        ),
        out_specs=(P("cam", "pts", None), P("cam", "pts", None)),
        check_vma=False,
    )
```

```python
import functools

import jax
import jax.numpy as jnp
from jax import lax
from jax.experimental import pallas as pl
from jax.experimental.pallas import tpu as pltpu
from jax.sharding import PartitionSpec as P

ITERS = 3
CPAR = 9
CAMS = 64
LANES = 128
SCALE = 0.125
TOG = 16
MESH = pl.DeviceIdType.MESH
F32 = jnp.float32
BF16 = jnp.bfloat16
NT = (((1,), (1,)), ((), ()))
NN = (((1,), (0,)), ((), ()))


def mm(a, b, dims):
    return lax.dot_general(a, b, dims, preferred_element_type=F32)


def split_two(x):
    hi = x.astype(BF16)
    return hi, (x - hi.astype(F32)).astype(BF16)


def kernel(
    n_pts, n_cam, tiles, slots, ct,
    rhs_ref, damp_ref, precond_ref, ids_ref, counts_ref,
    cam_jac_ref, pt_jac_ref, damp_pt_ref, cam_index_ref,
    out_ref,
    jac, pjac, dpt, cidx, inv, sel, pick_hot, sum_hot, picked, spread, win_split, found, given_split,
    win, acc, got, mixed, parts, vecs, bases, scal_cam, scal_pts,
    in_sem, wsend, wrecv, fsend, frecv, psend, precv, rsend, rrecv, csend, crecv, osend, orecv,
):
    half = n_pts // 2
    chips = half * n_cam
    reach = half // 2
    span = 2 * reach + 1
    rows = span * 2 * ct
    width = 5 * LANES
    used = CPAR * CAMS * ct // LANES
    pairs = tiles * slots
    d = lax.axis_index("pts")
    g = lax.axis_index("cam")
    core = lax.rem(d, 2)
    other = 1 - core
    chip = g * half + d // 2

    def at_offset(offset):
        place = lax.rem(chip + (offset + chips), chips)
        return {"pts": lax.rem(place, half) * 2 + core, "cam": place // half}

    twin = {"pts": d + 1 - 2 * core, "cam": g}
    offsets = []
    for far in range(reach, 0, -1):
        offsets += [far, -far]
    places = {offset: at_offset(offset) for offset in offsets}

    loads = [
        pltpu.make_async_copy(pt_jac_ref.at[0], pjac, in_sem.at[0]),
        pltpu.make_async_copy(damp_pt_ref.at[0], dpt, in_sem.at[1]),
        pltpu.make_async_copy(cam_index_ref.at[0], cidx.at[pl.ds(0, tiles)], in_sem.at[2]),
        pltpu.make_async_copy(cam_jac_ref.at[0], jac, in_sem.at[3]),
    ]
    for load in loads:
        load.start()

    barrier = pltpu.get_barrier_semaphore()

    def greet(device):
        pl.semaphore_signal(barrier, inc=1, device_id=device, device_id_type=MESH)

    for offset in offsets:
        greet(places[offset])
    for i in range(1, n_cam):
        greet({"pts": d, "cam": lax.rem(g + i, n_cam)})
    for i in range(1, n_pts):
        greet({"pts": lax.rem(d + i, n_pts), "cam": g})

    tail = []

    pl.semaphore_wait(barrier, len(offsets) + (n_cam - 1) + (n_pts - 1))

    def send(src, dst, ssem, rsem, device):
        copy = pltpu.make_async_remote_copy(
            src_ref=src, dst_ref=dst, send_sem=ssem, recv_sem=rsem, device_id=device, device_id_type=MESH
        )
        copy.start()
        tail.append(copy)
        return copy

    def drain(keep):
        waiting = [copy for copy in tail if all(copy is not kept for kept in keep)]
        tail[:] = keep
        for copy in waiting:
            copy.wait_send()

    def block(ref, *index):
        return ref.at[(*index, pl.ds(0, used))]

    def start_gather(p, value):
        win[p, reach, core] = value
        own = block(win, p, reach, core)
        copies = []
        for offset in offsets:
            slot = reach - offset
            copies.append(send(own, block(win, p, slot, core), wsend.at[p, slot], wrecv.at[p, slot], places[offset]))
        copies.append(send(own, own, fsend.at[p, reach], frecv.at[p, reach], twin))
        return copies

    def finish_gather(p, copies):
        forwards = [copies.pop()]
        drain(copies + forwards)
        for offset, copy in list(zip(offsets, copies)):
            copy.wait_recv()
            slot = reach - offset
            here = block(win, p, slot, core)
            forwards.append(send(here, here, fsend.at[p, slot], frecv.at[p, slot], twin))
        for copy in forwards:
            copy.wait_recv()

    def reduce_blocks(p, keep, meanwhile):
        swaps = []
        order = offsets + [0]
        for offset in order:
            b = reach + offset
            swaps.append(send(block(acc, p, b, other), block(got, p, b), psend.at[p, b], precv.at[p, b], twin))
        drain(swaps + keep)
        copies = []
        for offset, swap in zip(order, swaps):
            b = reach + offset
            swap.wait_recv()
            total = acc[p, b, core] + got[p, b]
            if offset:
                mixed[p, b] = total
                copies.append(
                    send(block(mixed, p, b), block(parts, p, b), rsend.at[p, b], rrecv.at[p, b], places[offset])
                )
        meanwhile()
        for offset, copy in zip(offsets, copies):
            copy.wait_recv()
            total = total + parts[p, reach + offset]
        return jnp.where(filled, total, 0.0)

    sub = lax.broadcasted_iota(jnp.int32, (slots, LANES), 0)
    lane = lax.broadcasted_iota(jnp.int32, (slots, LANES), 1)
    low = lane < CAMS
    early = lax.rem(sub, 4) < 2
    aligned = early == low
    top = sub < 4
    filled = lax.broadcasted_iota(jnp.int32, (5 * ct, LANES), 0) < used

    def pack_last(x):
        return jnp.where(low, x, pltpu.roll(pltpu.roll(x, 4, 0), CAMS, 1))

    def unpack_last(x):
        return jnp.where(top, x, pltpu.roll(pltpu.roll(x, 4, 0), CAMS, 1))

    def packed(value):
        groups = [value[:, n * LANES : (n + 1) * LANES] for n in range(4)]
        ending = jnp.concatenate([value[:, 4 * LANES :], jnp.zeros((ct, CAMS), F32)], axis=1)
        return jnp.concatenate(groups + [jnp.where(top, pack_last(ending), 0.0)], axis=0)

    def unpacked(value):
        groups = [value[n * ct : (n + 1) * ct] for n in range(4)]
        return jnp.concatenate(groups + [unpack_last(value[4 * ct :])[:, :CAMS]], axis=1)

    rhs = packed(rhs_ref[0])
    damp = packed(damp_ref[0])
    precond = packed(precond_ref[0])
    vecs[0] = rhs
    scaled = precond * rhs
    bases[0] = scaled
    copies = start_gather(0, scaled)
    shift = (d // 2) * (2 * ct)
    spot = lax.broadcasted_iota(jnp.int32, (slots, width), 1)
    spot = jnp.where(spot < rows, spot, spot - rows)
    ids = jnp.concatenate([ids_ref[0] - shift, jnp.zeros((slots, LANES - tiles), jnp.int32)], axis=1)

    def pick_rows(i, carry):
        hots = []
        for u in range(2):
            own = jnp.take_along_axis(ids, jnp.full_like(ids, 2 * i + u), axis=1, mode="promise_in_bounds")
            hots.append(jnp.where(spot == own[:, :1], 1.0, 0.0))
        pick_hot[pl.ds(pl.multiple_of(i * 16, 16), 16), :] = jnp.concatenate(hots, axis=0).astype(BF16)
        return carry

    lax.fori_loop(0, pairs // 16, pick_rows, 0)
    for i in range(pairs // LANES):
        hot = pick_hot[pl.ds(i * LANES, LANES), pl.ds(0, 3 * LANES)].astype(F32)
        hot = jnp.transpose(hot)[:rows].astype(BF16)
        sum_hot[:, pl.ds(i * LANES, LANES)] = hot
        sum_hot[:, pl.ds(pairs + i * LANES, LANES)] = hot

    loads[0].wait()
    loads[1].wait()
    loads[2].wait()
    loads[3].wait()
    def live_of(t):
        return sub < counts_ref[0, t]

    def point_rows(t):
        return [pjac[t, r] for r in range(6)]

    camera = lax.broadcasted_iota(jnp.int32, (CAMS, LANES), 0)

    def prepare(i, carry):
        sums = [[] for _ in range(6)]
        for u in range(8):
            t = i * 8 + u
            live = live_of(t)
            p = [jnp.where(live, row, 0.0) for row in point_rows(t)]
            for r in range(2 * CPAR):
                jac[t, r] = jnp.where(live, jac[t, r], 0.0)
            for n, (a, b) in enumerate(((0, 0), (0, 1), (0, 2), (1, 1), (1, 2), (2, 2))):
                sums[n].append(jnp.sum(p[a] * p[b] + p[3 + a] * p[3 + b], axis=0, keepdims=True))
            for k in range(slots):
                index = cidx[t, pl.ds(k, 1), :]
                hot = jnp.where(camera == index, 1.0, 0.0).astype(BF16)
                sel[TOG + t, pl.ds((k // 2) * CAMS, CAMS), pl.ds((k % 2) * LANES, LANES)] = hot
        here = pl.ds(pl.multiple_of(i * 8, 8), 8)
        v00, v01, v02, v11, v12, v22 = [jnp.concatenate(part, axis=0) for part in sums]
        v00 = v00 + dpt[0, here, :]
        v11 = v11 + dpt[1, here, :]
        v22 = v22 + dpt[2, here, :]
        c00 = v11 * v22 - v12 * v12
        c01 = v12 * v02 - v01 * v22
        c02 = v01 * v12 - v11 * v02
        c11 = v22 * v00 - v02 * v02
        c12 = v02 * v01 - v00 * v12
        c22 = v00 * v11 - v01 * v01
        det = v00 * c00 + v01 * c01 + v02 * c02
        for n, value in enumerate((c00, c01, c02, c11, c12, c22)):
            inv[n, here, :] = value / det
        return carry

    lax.fori_loop(0, tiles // 8, prepare, 0)

    together = TOG
    lower = 80
    parity = lax.rem(lax.broadcasted_iota(jnp.int32, (CPAR * slots, LANES), 0), 2)
    odd_rows = parity.astype(F32).astype(BF16)
    even_rows = (1 - parity).astype(F32).astype(BF16)
    for u in range(together):
        cidx[tiles + u] = jnp.zeros((slots, LANES), jnp.int32)
        given_split[u] = jnp.zeros((2 * lower, 2 * LANES), BF16)

    def look_up(t, u):
        index = cidx[t]
        for first in range(2):
            for j in range(first, CPAR, 2):
                table = picked[pl.ds(t * slots, slots), pl.ds((j // 2) * LANES, LANES)]
                found[u, j] = jnp.take_along_axis(table, index + CAMS * first, axis=1, mode="promise_in_bounds")

    def observe(t, u):
        j_rows = [jac[t, r] for r in range(2 * CPAR)]
        p = point_rows(t)
        q = []
        for r in range(2):
            total = j_rows[CPAR * r] * found[u, 0]
            for j in range(1, CPAR):
                total = total + j_rows[CPAR * r + j] * found[u, j]
            q.append(total)
        y = [jnp.sum(p[a] * q[0] + p[3 + a] * q[1], axis=0, keepdims=True) for a in range(3)]
        m = [inv[n, pl.ds(t, 1), :] for n in range(6)]
        z = [
            m[0] * y[0] + m[1] * y[1] + m[2] * y[2],
            m[1] * y[0] + m[3] * y[1] + m[4] * y[2],
            m[2] * y[0] + m[4] * y[1] + m[5] * y[2],
        ]
        e = []
        for r in range(2):
            back = p[3 * r] * z[0] + p[3 * r + 1] * z[1] + p[3 * r + 2] * z[2]
            e.append(q[r] - back)
        given = jnp.concatenate([j_rows[j] * e[0] + j_rows[CPAR + j] * e[1] for j in range(CPAR)], axis=0)
        hi, lo = split_two(given)
        heights = CPAR * slots
        given_split[u, pl.ds(0, heights), :] = jnp.concatenate([hi * even_rows, hi * odd_rows], axis=1)
        given_split[u, pl.ds(lower, heights), :] = jnp.concatenate([lo * even_rows, lo * odd_rows], axis=1)
        return q[0] * e[0] + q[1] * e[1]

    def camera_sums(t, u):
        out = mm(given_split[u], sel[t], NT)

        def diagonal(j):
            both = []
            for n in range(slots // 4):
                cut = slice(n * LANES, (n + 1) * LANES)
                both.append(
                    out[j * slots : (j + 1) * slots, cut] + out[lower + j * slots : lower + (j + 1) * slots, cut]
                )
            return jnp.where(top, both[0], both[1])

        merged = []
        for i in range(0, CPAR, 2):
            first = diagonal(i)
            second = diagonal(i + 1) if i + 1 < CPAR else jnp.zeros_like(first)
            turned = pltpu.roll(jnp.where(early, second, first), CAMS, 1)
            merged.append(jnp.where(aligned, jnp.where(early, first, second), turned))
        return jnp.concatenate(merged, axis=1)

    steps = tiles // together

    def look_step(i):
        for u in range(together):
            look_up(i * together + u, u)

    def observe_step(i, bend):
        for u in range(together):
            bend = bend + observe(i * together + u, u)
        return bend

    def sum_step(i):
        terms = [camera_sums(i * together + u, u) for u in range(together)]
        for u in range(0, together, 2):
            hi, lo = split_two(jnp.concatenate(terms[u : u + 2], axis=0))
            start = pl.multiple_of((i * together + u) * slots, 16)
            spread[0, pl.ds(start, 16), :] = hi
            spread[1, pl.ds(start, 16), :] = lo

    def all_steps(i, bend):
        sum_step(i)
        bend = observe_step(i, bend)
        look_step(i + 1)
        return bend

    wanted = [(i, j) for j in range(ITERS) for i in range(j + 1)]

    def lane_sums(product):
        line = product[:ct]
        for n in range(1, 5):
            line = line + product[n * ct : (n + 1) * ct]
        return line

    def start_sums(bend):
        lines = [lane_sums(bases[i] * vecs[j]) for i, j in wanted]
        last = bases[ITERS - 1]
        lines.append(SCALE * (bend + lane_sums(damp * last * last)))
        lines = [jnp.sum(line, axis=0, keepdims=True) for line in lines]
        lines.append(jnp.zeros((8 - len(lines), LANES), F32))
        scal_cam[g] = jnp.concatenate(lines, axis=0)
        return [
            send(scal_cam.at[g], scal_cam.at[g], csend.at[i], crecv.at[i], {"pts": d, "cam": lax.rem(g + i, n_cam)})
            for i in range(1, n_cam)
        ]

    def cross_sums(copies):
        for copy in copies:
            copy.wait_recv()
        total = scal_cam[0]
        for i in range(1, n_cam):
            total = total + scal_cam[i]
        scal_pts[d] = total
        return [
            send(scal_pts.at[d], scal_pts.at[d], osend.at[i], orecv.at[i], {"pts": lax.rem(d + i, n_pts), "cam": g})
            for i in range(1, n_pts)
        ]

    for p in range(ITERS):
        finish_gather(p, copies)
        for n in range(5):
            window = win[p, :, :, pl.ds(n * ct, ct), :].reshape(rows, LANES)
            if n == 4:
                window = jnp.concatenate(
                    [unpack_last(window[i * ct : (i + 1) * ct]) for i in range(2 * span)], axis=0
                )
            hi, lo = split_two(window)
            cut = pl.ds(n * LANES, LANES)
            win_split[pl.ds(0, rows), cut] = hi
            win_split[pl.ds(rows, rows), cut] = lo

        def pick(i, carry):
            here = pl.ds(pl.multiple_of(i * (pairs // 2), 16), pairs // 2)
            picked[here, :] = mm(pick_hot[here, pl.ds(0, 2 * rows)], win_split[...], NN)
            return carry

        lax.fori_loop(0, 2, pick, 0)
        look_step(0)
        bend = lax.fori_loop(0, steps, all_steps, jnp.zeros((slots, LANES), F32))
        sum_step(steps)
        if p + 1 == ITERS:
            started = start_sums(bend)
        for low_group, high_group in ((0, 2), (2, 4), (4, 5)):
            cut = pl.ds(low_group * LANES, (high_group - low_group) * LANES)
            given = jnp.concatenate([spread[n, pl.ds(TOG * slots, pairs), cut] for n in range(2)], axis=0)
            sums = mm(sum_hot[...], given, NN)
            for i in range(low_group, high_group):
                value = sums[:, (i - low_group) * LANES : (i - low_group + 1) * LANES]
                if i == 4:
                    value = jnp.concatenate(
                        [pack_last(value[n * ct : (n + 1) * ct]) for n in range(2 * span)], axis=0
                    )
                acc[p, :, :, pl.ds(i * ct, ct), :] = value.reshape(span, 2, ct, LANES)
        crossing = []

        def meanwhile():
            if p + 1 == ITERS:
                crossing.extend(cross_sums(started))

        total = reduce_blocks(p, started if p + 1 == ITERS else [], meanwhile)
        mapped = SCALE * (total + damp * bases[p])
        vecs[p + 1] = mapped
        if p + 1 < ITERS:
            scaled = precond * mapped
            bases[p + 1] = scaled
            copies = start_gather(p + 1, scaled)

    for copy in crossing:
        copy.wait_recv()
    total = scal_pts[0]
    for i in range(1, n_pts):
        total = total + scal_pts[i]
    sums = jnp.broadcast_to(jnp.sum(total, axis=1, keepdims=True), (8, LANES))
    gram = {}
    for i, (a, b) in enumerate(wanted):
        gram[a, b] = gram[b, a] = sums[i : i + 1, :]
    for i in range(ITERS - 1):
        gram[i, ITERS] = gram[i + 1, ITERS - 1]
    gram[ITERS - 1, ITERS] = sums[len(wanted) : len(wanted) + 1, :]

    one = jnp.ones((1, LANES), F32)
    nil = jnp.zeros((1, LANES), F32)
    x = [nil] * ITERS
    r = [one] + [nil] * ITERS
    s = [one] + [nil] * (ITERS - 1)
    energy = gram[0, 0]
    for p in range(ITERS):
        mapped = [nil] + [value * (1.0 / SCALE) for value in s]
        steep = nil
        for i in range(p + 1):
            row = nil
            for j in range(1, p + 2):
                row = row + mapped[j] * gram[i, j]
            steep = steep + s[i] * row
        step = energy / steep
        x = [a + step * b for a, b in zip(x, s)]
        r = [a - step * b for a, b in zip(r, mapped)]
        if p + 1 < ITERS:
            following = nil
            for i in range(p + 2):
                row = nil
                for j in range(p + 2):
                    row = row + r[j] * gram[i, j]
                following = following + r[i] * row
            ratio = following / energy
            s = [a + ratio * b for a, b in zip(r[:ITERS], s)]
            energy = following

    def spread_out(value):
        return jnp.broadcast_to(value, (5 * ct, LANES))

    solution_value = spread_out(x[0]) * bases[0]
    residual_value = spread_out(r[0]) * vecs[0]
    for i in range(1, ITERS):
        solution_value = solution_value + spread_out(x[i]) * bases[i]
    for i in range(1, ITERS + 1):
        residual_value = residual_value + spread_out(r[i]) * vecs[i]
    drain([])
    out_ref[0] = unpacked(solution_value)
    out_ref[1] = unpacked(residual_value)


def solution(mesh):
    n_pts, n_cam = mesh.shape["pts"], mesh.shape["cam"]

    def on_device(rhs, damp_cam, precond, cam_jac, pt_jac, damp_pt, cam_index, tile_ids, counts):
        ct = rhs.shape[1]
        tiles, slots = cam_jac.shape[1:3]
        pairs = tiles * slots
        span = n_pts // 2 + 1
        rows = span * 2 * ct
        width = 5 * LANES
        vmem = pl.BlockSpec(memory_space=pltpu.VMEM)
        anywhere = pl.BlockSpec(memory_space=pl.ANY)
        dma = pltpu.SemaphoreType.DMA
        both = pl.pallas_call(
            functools.partial(kernel, n_pts, n_cam, tiles, slots, ct),
            out_shape=jax.ShapeDtypeStruct((2, *rhs.shape[1:]), F32),
            in_specs=[vmem] * 4 + [pl.BlockSpec(memory_space=pltpu.SMEM)] + [anywhere] * 4,
            out_specs=vmem,
            scratch_shapes=[
                pltpu.VMEM((tiles, 2 * CPAR, slots, LANES), F32),
                pltpu.VMEM((tiles, 6, slots, LANES), F32),
                pltpu.VMEM((3, tiles, LANES), F32),
                pltpu.VMEM((tiles + TOG, slots, LANES), jnp.int32),
                pltpu.VMEM((6, tiles, LANES), F32),
                pltpu.VMEM((TOG + tiles, slots * CAMS // 2, 2 * LANES), BF16),
                pltpu.VMEM((pairs, width), BF16),
                pltpu.VMEM((rows, 2 * pairs), BF16),
                pltpu.VMEM((pairs + TOG * slots, width), F32),
                pltpu.VMEM((2, TOG * slots + pairs, width), BF16),
                pltpu.VMEM((2 * rows, width), BF16),
                pltpu.VMEM((TOG, CPAR, slots, LANES), F32),
                pltpu.VMEM((TOG, 160, 2 * LANES), BF16),
                pltpu.VMEM((ITERS, span, 2, 5 * ct, LANES), F32),
                pltpu.VMEM((ITERS, span, 2, 5 * ct, LANES), F32),
                pltpu.VMEM((ITERS, span, 5 * ct, LANES), F32),
                pltpu.VMEM((ITERS, span, 5 * ct, LANES), F32),
                pltpu.VMEM((ITERS, span, 5 * ct, LANES), F32),
                pltpu.VMEM((ITERS + 1, 5 * ct, LANES), F32),
                pltpu.VMEM((ITERS, 5 * ct, LANES), F32),
                pltpu.VMEM((n_cam, 8, LANES), F32),
                pltpu.VMEM((n_pts, 8, LANES), F32),
                dma((4,)),
            ]
            + [dma((ITERS, span))] * 8
            + [dma((n_cam,)), dma((n_cam,)), dma((n_pts,)), dma((n_pts,))],
            compiler_params=pltpu.CompilerParams(
                collective_id=0, has_side_effects=True, vmem_limit_bytes=62_000_000
            ),
        )(
            rhs, damp_cam, precond, jnp.swapaxes(tile_ids, 1, 2), counts,
            jnp.swapaxes(cam_jac, 2, 3), jnp.swapaxes(pt_jac, 2, 3), jnp.swapaxes(damp_pt, 1, 2), cam_index,
        )
        return both[:1], both[1:]

    return jax.shard_map(
        on_device,
        mesh=mesh,
        in_specs=(
            P("cam", "pts", None),
            P("cam", "pts", None),
            P("cam", "pts", None),
            P("cam", "pts", None, None, None),
            P("cam", "pts", None, None, None),
            P("cam", "pts", None, None),
            P("cam", "pts", None, None),
            P("cam", "pts", None),
            P("cam", "pts"),
        ),
        out_specs=(P("cam", "pts", None), P("cam", "pts", None)),
        check_vma=False,
    )
```

```python
import functools

import jax
import jax.numpy as jnp
from jax import lax
from jax.experimental import pallas as pl
from jax.experimental.pallas import tpu as pltpu
from jax.sharding import PartitionSpec as P

ITERS = 3
CPAR = 9
CAMS = 64
LANES = 128
SCALE = 0.125
TOG = 24
MESH = pl.DeviceIdType.MESH
F32 = jnp.float32
BF16 = jnp.bfloat16
NT = (((1,), (1,)), ((), ()))
NN = (((1,), (0,)), ((), ()))


def mm(a, b, dims):
    return lax.dot_general(a, b, dims, preferred_element_type=F32)


def split_two(x):
    hi = x.astype(BF16)
    return hi, (x - hi.astype(F32)).astype(BF16)


def kernel(
    n_pts, n_cam, tiles, slots, ct,
    rhs_ref, damp_ref, precond_ref, ids_ref, counts_ref,
    cam_jac_ref, pt_jac_ref, damp_pt_ref, cam_index_ref,
    out_ref,
    jac, pjac, dpt, cidx, inv, sel, pick_hot, sum_hot, picked, spread, win_split, found, given_split,
    win, acc, got, mixed, parts, vecs, bases, scal_cam, scal_pts,
    in_sem, wsend, wrecv, fsend, frecv, psend, precv, rsend, rrecv, csend, crecv, osend, orecv,
):
    half = n_pts // 2
    chips = half * n_cam
    reach = half // 2
    span = 2 * reach + 1
    rows = span * 2 * ct
    width = 5 * LANES
    used = CPAR * CAMS * ct // LANES
    pairs = tiles * slots
    d = lax.axis_index("pts")
    g = lax.axis_index("cam")
    core = lax.rem(d, 2)
    other = 1 - core
    chip = g * half + d // 2

    def at_offset(offset):
        place = lax.rem(chip + (offset + chips), chips)
        return {"pts": lax.rem(place, half) * 2 + core, "cam": place // half}

    twin = {"pts": d + 1 - 2 * core, "cam": g}
    offsets = []
    for far in range(reach, 0, -1):
        offsets += [far, -far]
    places = {offset: at_offset(offset) for offset in offsets}

    loads = [
        pltpu.make_async_copy(pt_jac_ref.at[0], pjac, in_sem.at[0]),
        pltpu.make_async_copy(damp_pt_ref.at[0], dpt, in_sem.at[1]),
        pltpu.make_async_copy(cam_index_ref.at[0], cidx.at[pl.ds(0, tiles)], in_sem.at[2]),
        pltpu.make_async_copy(cam_jac_ref.at[0], jac, in_sem.at[3]),
    ]
    for load in loads:
        load.start()

    barrier = pltpu.get_barrier_semaphore()

    def greet(device):
        pl.semaphore_signal(barrier, inc=1, device_id=device, device_id_type=MESH)

    for offset in offsets:
        greet(places[offset])
    for i in range(1, n_cam):
        greet({"pts": d, "cam": lax.rem(g + i, n_cam)})
    for i in range(1, n_pts):
        greet({"pts": lax.rem(d + i, n_pts), "cam": g})

    tail = []

    pl.semaphore_wait(barrier, len(offsets) + (n_cam - 1) + (n_pts - 1))

    def send(src, dst, ssem, rsem, device):
        copy = pltpu.make_async_remote_copy(
            src_ref=src, dst_ref=dst, send_sem=ssem, recv_sem=rsem, device_id=device, device_id_type=MESH
        )
        copy.start()
        tail.append(copy)
        return copy

    def drain(keep):
        waiting = [copy for copy in tail if all(copy is not kept for kept in keep)]
        tail[:] = keep
        for copy in waiting:
            copy.wait_send()

    def block(ref, *index):
        return ref.at[(*index, pl.ds(0, used))]

    def start_gather(p, value):
        win[p, reach, core] = value
        own = block(win, p, reach, core)
        copies = []
        for offset in offsets:
            slot = reach - offset
            copies.append(send(own, block(win, p, slot, core), wsend.at[p, slot], wrecv.at[p, slot], places[offset]))
        copies.append(send(own, own, fsend.at[p, reach], frecv.at[p, reach], twin))
        return copies

    def finish_gather(p, copies):
        forwards = [copies.pop()]
        drain(copies + forwards)
        for offset, copy in list(zip(offsets, copies)):
            copy.wait_recv()
            slot = reach - offset
            here = block(win, p, slot, core)
            forwards.append(send(here, here, fsend.at[p, slot], frecv.at[p, slot], twin))
        for copy in forwards:
            copy.wait_recv()

    def reduce_blocks(p, keep, meanwhile):
        swaps = []
        order = offsets + [0]
        for offset in order:
            b = reach + offset
            swaps.append(send(block(acc, p, b, other), block(got, p, b), psend.at[p, b], precv.at[p, b], twin))
        drain(swaps + keep)
        copies = []
        for offset, swap in zip(order, swaps):
            b = reach + offset
            swap.wait_recv()
            total = acc[p, b, core] + got[p, b]
            if offset:
                mixed[p, b] = total
                copies.append(
                    send(block(mixed, p, b), block(parts, p, b), rsend.at[p, b], rrecv.at[p, b], places[offset])
                )
        meanwhile()
        for offset, copy in zip(offsets, copies):
            copy.wait_recv()
            total = total + parts[p, reach + offset]
        return jnp.where(filled, total, 0.0)

    sub = lax.broadcasted_iota(jnp.int32, (slots, LANES), 0)
    lane = lax.broadcasted_iota(jnp.int32, (slots, LANES), 1)
    low = lane < CAMS
    early = lax.rem(sub, 4) < 2
    aligned = early == low
    top = sub < 4
    filled = lax.broadcasted_iota(jnp.int32, (5 * ct, LANES), 0) < used

    def pack_last(x):
        return jnp.where(low, x, pltpu.roll(pltpu.roll(x, 4, 0), CAMS, 1))

    def unpack_last(x):
        return jnp.where(top, x, pltpu.roll(pltpu.roll(x, 4, 0), CAMS, 1))

    def packed(value):
        groups = [value[:, n * LANES : (n + 1) * LANES] for n in range(4)]
        ending = jnp.concatenate([value[:, 4 * LANES :], jnp.zeros((ct, CAMS), F32)], axis=1)
        return jnp.concatenate(groups + [jnp.where(top, pack_last(ending), 0.0)], axis=0)

    def unpacked(value):
        groups = [value[n * ct : (n + 1) * ct] for n in range(4)]
        return jnp.concatenate(groups + [unpack_last(value[4 * ct :])[:, :CAMS]], axis=1)

    rhs = packed(rhs_ref[0])
    damp = packed(damp_ref[0])
    precond = packed(precond_ref[0])
    vecs[0] = rhs
    scaled = precond * rhs
    bases[0] = scaled
    copies = start_gather(0, scaled)
    shift = (d // 2) * (2 * ct)
    spot = lax.broadcasted_iota(jnp.int32, (slots, width), 1)
    spot = jnp.where(spot < rows, spot, spot - rows)
    ids = jnp.concatenate([ids_ref[0] - shift, jnp.zeros((slots, LANES - tiles), jnp.int32)], axis=1)

    def pick_rows(i, carry):
        hots = []
        for u in range(2):
            own = jnp.take_along_axis(ids, jnp.full_like(ids, 2 * i + u), axis=1, mode="promise_in_bounds")
            hots.append(jnp.where(spot == own[:, :1], 1.0, 0.0))
        pick_hot[pl.ds(pl.multiple_of(i * 16, 16), 16), :] = jnp.concatenate(hots, axis=0).astype(BF16)
        return carry

    lax.fori_loop(0, pairs // 16, pick_rows, 0)
    for i in range(pairs // LANES):
        hot = pick_hot[pl.ds(i * LANES, LANES), pl.ds(0, 3 * LANES)].astype(F32)
        hot = jnp.transpose(hot)[:rows].astype(BF16)
        sum_hot[:, pl.ds(i * LANES, LANES)] = hot
        sum_hot[:, pl.ds(pairs + i * LANES, LANES)] = hot

    loads[0].wait()
    loads[1].wait()
    loads[2].wait()
    loads[3].wait()
    def live_of(t):
        return sub < counts_ref[0, t]

    def point_rows(t):
        return [pjac[t, r] for r in range(6)]

    camera = lax.broadcasted_iota(jnp.int32, (CAMS, LANES), 0)

    def prepare(i, carry):
        sums = [[] for _ in range(6)]
        for u in range(8):
            t = i * 8 + u
            live = live_of(t)
            p = [jnp.where(live, row, 0.0) for row in point_rows(t)]
            for r in range(2 * CPAR):
                jac[t, r] = jnp.where(live, jac[t, r], 0.0)
            for n, (a, b) in enumerate(((0, 0), (0, 1), (0, 2), (1, 1), (1, 2), (2, 2))):
                sums[n].append(jnp.sum(p[a] * p[b] + p[3 + a] * p[3 + b], axis=0, keepdims=True))
            for k in range(slots):
                index = cidx[t, pl.ds(k, 1), :]
                hot = jnp.where(camera == index, 1.0, 0.0).astype(BF16)
                sel[TOG + t, pl.ds((k // 2) * CAMS, CAMS), pl.ds((k % 2) * LANES, LANES)] = hot
        here = pl.ds(pl.multiple_of(i * 8, 8), 8)
        v00, v01, v02, v11, v12, v22 = [jnp.concatenate(part, axis=0) for part in sums]
        v00 = v00 + dpt[0, here, :]
        v11 = v11 + dpt[1, here, :]
        v22 = v22 + dpt[2, here, :]
        c00 = v11 * v22 - v12 * v12
        c01 = v12 * v02 - v01 * v22
        c02 = v01 * v12 - v11 * v02
        c11 = v22 * v00 - v02 * v02
        c12 = v02 * v01 - v00 * v12
        c22 = v00 * v11 - v01 * v01
        det = v00 * c00 + v01 * c01 + v02 * c02
        for n, value in enumerate((c00, c01, c02, c11, c12, c22)):
            inv[n, here, :] = value / det
        return carry

    lax.fori_loop(0, tiles // 8, prepare, 0)

    together = TOG
    lower = 80
    parity = lax.rem(lax.broadcasted_iota(jnp.int32, (CPAR * slots, LANES), 0), 2)
    odd_rows = parity.astype(F32).astype(BF16)
    even_rows = (1 - parity).astype(F32).astype(BF16)
    for u in range(together):
        cidx[tiles + u] = jnp.zeros((slots, LANES), jnp.int32)
        given_split[u] = jnp.zeros((2 * lower, 2 * LANES), BF16)

    def look_up(t, u):
        index = cidx[t]
        for first in range(2):
            for j in range(first, CPAR, 2):
                table = picked[pl.ds(t * slots, slots), pl.ds((j // 2) * LANES, LANES)]
                found[u, j] = jnp.take_along_axis(table, index + CAMS * first, axis=1, mode="promise_in_bounds")

    def observe(t, u):
        j_rows = [jac[t, r] for r in range(2 * CPAR)]
        p = point_rows(t)
        q = []
        for r in range(2):
            total = j_rows[CPAR * r] * found[u, 0]
            for j in range(1, CPAR):
                total = total + j_rows[CPAR * r + j] * found[u, j]
            q.append(total)
        y = [jnp.sum(p[a] * q[0] + p[3 + a] * q[1], axis=0, keepdims=True) for a in range(3)]
        m = [inv[n, pl.ds(t, 1), :] for n in range(6)]
        z = [
            m[0] * y[0] + m[1] * y[1] + m[2] * y[2],
            m[1] * y[0] + m[3] * y[1] + m[4] * y[2],
            m[2] * y[0] + m[4] * y[1] + m[5] * y[2],
        ]
        e = []
        for r in range(2):
            back = p[3 * r] * z[0] + p[3 * r + 1] * z[1] + p[3 * r + 2] * z[2]
            e.append(q[r] - back)
        given = jnp.concatenate([j_rows[j] * e[0] + j_rows[CPAR + j] * e[1] for j in range(CPAR)], axis=0)
        hi, lo = split_two(given)
        heights = CPAR * slots
        given_split[u, pl.ds(0, heights), :] = jnp.concatenate([hi * even_rows, hi * odd_rows], axis=1)
        given_split[u, pl.ds(lower, heights), :] = jnp.concatenate([lo * even_rows, lo * odd_rows], axis=1)
        return q[0] * e[0] + q[1] * e[1]

    def camera_sums(t, u):
        out = mm(given_split[u], sel[t], NT)

        def diagonal(j):
            both = []
            for n in range(slots // 4):
                cut = slice(n * LANES, (n + 1) * LANES)
                both.append(
                    out[j * slots : (j + 1) * slots, cut] + out[lower + j * slots : lower + (j + 1) * slots, cut]
                )
            return jnp.where(top, both[0], both[1])

        merged = []
        for i in range(0, CPAR, 2):
            first = diagonal(i)
            second = diagonal(i + 1) if i + 1 < CPAR else jnp.zeros_like(first)
            turned = pltpu.roll(jnp.where(early, second, first), CAMS, 1)
            merged.append(jnp.where(aligned, jnp.where(early, first, second), turned))
        return jnp.concatenate(merged, axis=1)

    steps = tiles // together

    def look_step(i):
        for u in range(together):
            look_up(i * together + u, u)

    def observe_step(i, bend):
        for u in range(together):
            bend = bend + observe(i * together + u, u)
        return bend

    def sum_step(i):
        terms = [camera_sums(i * together + u, u) for u in range(together)]
        for u in range(0, together, 2):
            hi, lo = split_two(jnp.concatenate(terms[u : u + 2], axis=0))
            start = pl.multiple_of((i * together + u) * slots, 16)
            spread[0, pl.ds(start, 16), :] = hi
            spread[1, pl.ds(start, 16), :] = lo

    def all_steps(i, bend):
        sum_step(i)
        bend = observe_step(i, bend)
        look_step(i + 1)
        return bend

    wanted = [(i, j) for j in range(ITERS) for i in range(j + 1)]

    def lane_sums(product):
        line = product[:ct]
        for n in range(1, 5):
            line = line + product[n * ct : (n + 1) * ct]
        return line

    def start_sums(bend):
        lines = [lane_sums(bases[i] * vecs[j]) for i, j in wanted]
        last = bases[ITERS - 1]
        lines.append(SCALE * (bend + lane_sums(damp * last * last)))
        lines = [jnp.sum(line, axis=0, keepdims=True) for line in lines]
        lines.append(jnp.zeros((8 - len(lines), LANES), F32))
        scal_cam[g] = jnp.concatenate(lines, axis=0)
        return [
            send(scal_cam.at[g], scal_cam.at[g], csend.at[i], crecv.at[i], {"pts": d, "cam": lax.rem(g + i, n_cam)})
            for i in range(1, n_cam)
        ]

    def cross_sums(copies):
        for copy in copies:
            copy.wait_recv()
        total = scal_cam[0]
        for i in range(1, n_cam):
            total = total + scal_cam[i]
        scal_pts[d] = total
        return [
            send(scal_pts.at[d], scal_pts.at[d], osend.at[i], orecv.at[i], {"pts": lax.rem(d + i, n_pts), "cam": g})
            for i in range(1, n_pts)
        ]

    for p in range(ITERS):
        finish_gather(p, copies)
        for n in range(5):
            window = win[p, :, :, pl.ds(n * ct, ct), :].reshape(rows, LANES)
            if n == 4:
                window = jnp.concatenate(
                    [unpack_last(window[i * ct : (i + 1) * ct]) for i in range(2 * span)], axis=0
                )
            hi, lo = split_two(window)
            cut = pl.ds(n * LANES, LANES)
            win_split[pl.ds(0, rows), cut] = hi
            win_split[pl.ds(rows, rows), cut] = lo

        def pick(i, carry):
            here = pl.ds(pl.multiple_of(i * pairs, 16), pairs)
            picked[here, :] = mm(pick_hot[here, pl.ds(0, 2 * rows)], win_split[...], NN)
            return carry

        lax.fori_loop(0, 1, pick, 0)
        look_step(0)
        bend = lax.fori_loop(0, steps, all_steps, jnp.zeros((slots, LANES), F32))
        sum_step(steps)
        if p + 1 == ITERS:
            started = start_sums(bend)
        for low_group, high_group in ((0, 2), (2, 4), (4, 5)):
            cut = pl.ds(low_group * LANES, (high_group - low_group) * LANES)
            given = jnp.concatenate([spread[n, pl.ds(TOG * slots, pairs), cut] for n in range(2)], axis=0)
            sums = mm(sum_hot[...], given, NN)
            for i in range(low_group, high_group):
                value = sums[:, (i - low_group) * LANES : (i - low_group + 1) * LANES]
                if i == 4:
                    value = jnp.concatenate(
                        [pack_last(value[n * ct : (n + 1) * ct]) for n in range(2 * span)], axis=0
                    )
                acc[p, :, :, pl.ds(i * ct, ct), :] = value.reshape(span, 2, ct, LANES)
        crossing = []

        def meanwhile():
            if p + 1 == ITERS:
                crossing.extend(cross_sums(started))

        total = reduce_blocks(p, started if p + 1 == ITERS else [], meanwhile)
        mapped = SCALE * (total + damp * bases[p])
        vecs[p + 1] = mapped
        if p + 1 < ITERS:
            scaled = precond * mapped
            bases[p + 1] = scaled
            copies = start_gather(p + 1, scaled)

    for copy in crossing:
        copy.wait_recv()
    total = scal_pts[0]
    for i in range(1, n_pts):
        total = total + scal_pts[i]
    sums = jnp.broadcast_to(jnp.sum(total, axis=1, keepdims=True), (8, LANES))
    gram = {}
    for i, (a, b) in enumerate(wanted):
        gram[a, b] = gram[b, a] = sums[i : i + 1, :]
    for i in range(ITERS - 1):
        gram[i, ITERS] = gram[i + 1, ITERS - 1]
    gram[ITERS - 1, ITERS] = sums[len(wanted) : len(wanted) + 1, :]

    one = jnp.ones((1, LANES), F32)
    nil = jnp.zeros((1, LANES), F32)
    x = [nil] * ITERS
    r = [one] + [nil] * ITERS
    s = [one] + [nil] * (ITERS - 1)
    energy = gram[0, 0]
    for p in range(ITERS):
        mapped = [nil] + [value * (1.0 / SCALE) for value in s]
        steep = nil
        for i in range(p + 1):
            row = nil
            for j in range(1, p + 2):
                row = row + mapped[j] * gram[i, j]
            steep = steep + s[i] * row
        step = energy / steep
        x = [a + step * b for a, b in zip(x, s)]
        r = [a - step * b for a, b in zip(r, mapped)]
        if p + 1 < ITERS:
            following = nil
            for i in range(p + 2):
                row = nil
                for j in range(p + 2):
                    row = row + r[j] * gram[i, j]
                following = following + r[i] * row
            ratio = following / energy
            s = [a + ratio * b for a, b in zip(r[:ITERS], s)]
            energy = following

    def spread_out(value):
        return jnp.broadcast_to(value, (5 * ct, LANES))

    solution_value = spread_out(x[0]) * bases[0]
    residual_value = spread_out(r[0]) * vecs[0]
    for i in range(1, ITERS):
        solution_value = solution_value + spread_out(x[i]) * bases[i]
    for i in range(1, ITERS + 1):
        residual_value = residual_value + spread_out(r[i]) * vecs[i]
    drain([])
    out_ref[0] = unpacked(solution_value)
    out_ref[1] = unpacked(residual_value)


def solution(mesh):
    n_pts, n_cam = mesh.shape["pts"], mesh.shape["cam"]

    def on_device(rhs, damp_cam, precond, cam_jac, pt_jac, damp_pt, cam_index, tile_ids, counts):
        ct = rhs.shape[1]
        tiles, slots = cam_jac.shape[1:3]
        pairs = tiles * slots
        span = n_pts // 2 + 1
        rows = span * 2 * ct
        width = 5 * LANES
        vmem = pl.BlockSpec(memory_space=pltpu.VMEM)
        anywhere = pl.BlockSpec(memory_space=pl.ANY)
        dma = pltpu.SemaphoreType.DMA
        both = pl.pallas_call(
            functools.partial(kernel, n_pts, n_cam, tiles, slots, ct),
            out_shape=jax.ShapeDtypeStruct((2, *rhs.shape[1:]), F32),
            in_specs=[vmem] * 4 + [pl.BlockSpec(memory_space=pltpu.SMEM)] + [anywhere] * 4,
            out_specs=vmem,
            scratch_shapes=[
                pltpu.VMEM((tiles, 2 * CPAR, slots, LANES), F32),
                pltpu.VMEM((tiles, 6, slots, LANES), F32),
                pltpu.VMEM((3, tiles, LANES), F32),
                pltpu.VMEM((tiles + TOG, slots, LANES), jnp.int32),
                pltpu.VMEM((6, tiles, LANES), F32),
                pltpu.VMEM((TOG + tiles, slots * CAMS // 2, 2 * LANES), BF16),
                pltpu.VMEM((pairs, width), BF16),
                pltpu.VMEM((rows, 2 * pairs), BF16),
                pltpu.VMEM((pairs + TOG * slots, width), F32),
                pltpu.VMEM((2, TOG * slots + pairs, width), BF16),
                pltpu.VMEM((2 * rows, width), BF16),
                pltpu.VMEM((TOG, CPAR, slots, LANES), F32),
                pltpu.VMEM((TOG, 160, 2 * LANES), BF16),
                pltpu.VMEM((ITERS, span, 2, 5 * ct, LANES), F32),
                pltpu.VMEM((ITERS, span, 2, 5 * ct, LANES), F32),
                pltpu.VMEM((ITERS, span, 5 * ct, LANES), F32),
                pltpu.VMEM((ITERS, span, 5 * ct, LANES), F32),
                pltpu.VMEM((ITERS, span, 5 * ct, LANES), F32),
                pltpu.VMEM((ITERS + 1, 5 * ct, LANES), F32),
                pltpu.VMEM((ITERS, 5 * ct, LANES), F32),
                pltpu.VMEM((n_cam, 8, LANES), F32),
                pltpu.VMEM((n_pts, 8, LANES), F32),
                dma((4,)),
            ]
            + [dma((ITERS, span))] * 8
            + [dma((n_cam,)), dma((n_cam,)), dma((n_pts,)), dma((n_pts,))],
            compiler_params=pltpu.CompilerParams(
                collective_id=0, has_side_effects=True, vmem_limit_bytes=62_000_000
            ),
        )(
            rhs, damp_cam, precond, jnp.swapaxes(tile_ids, 1, 2), counts,
            jnp.swapaxes(cam_jac, 2, 3), jnp.swapaxes(pt_jac, 2, 3), jnp.swapaxes(damp_pt, 1, 2), cam_index,
        )
        return both[:1], both[1:]

    return jax.shard_map(
        on_device,
        mesh=mesh,
        in_specs=(
            P("cam", "pts", None),
            P("cam", "pts", None),
            P("cam", "pts", None),
            P("cam", "pts", None, None, None),
            P("cam", "pts", None, None, None),
            P("cam", "pts", None, None),
            P("cam", "pts", None, None),
            P("cam", "pts", None),
            P("cam", "pts"),
        ),
        out_specs=(P("cam", "pts", None), P("cam", "pts", None)),
        check_vma=False,
    )
```
